256 devices in a mesh: state: 8 (over z), tile: 32 (over x, y, core).
Axes of the slice: x: 4, y: 4, z: 8, core: 2. Of those that a mesh axis runs over, the one named last changes fastest.
Arguments:
- bands: bfloat16 [8, 240, 524288], P('state', None, 'tile')
- block_slot: int32 [8, 4096], P('state', 'tile'), may hold values from 0 to 7
- tile_counties: int32 [8, 256], P('state', 'tile'), may hold values from 0 to 383, as said below
- county_place: int32 [8, 384], P('state'), may hold values from 0 to 383, as said below
- label: int32 [8, 384], P('state', 'tile'), may hold values from -200 to 200
- w_first: bfloat16 [64, 240], replicated, may hold values from -0.375 to 0.375
- taps: float32 [3, 64], replicated, may hold values from -2 to 2
- w_second: bfloat16 [128, 64], replicated, may hold values from -0.75 to 0.75
- w_third: bfloat16 [128, 128], replicated, may hold values from -0.5 to 0.5
- w_head: bfloat16 [128], replicated, may hold values from -0.5 to 0.5
Outputs:
- county_mean: float32 [8, 384], P('state', 'tile')
- weight_grads: float32 [40256], replicated
The draws below stay inside these ranges and needn't reach their ends.
Inputs may be any that keep to these rules, and one draw needn't show every extreme that they name: `county_place`: each row is an ordering of the counties of one state region; the county at place p is owned by tile index p // 12 of that region. `tile_counties`: tile t's list names counties of its own state region owned by tile indices t, t + 1, ..., t + 4 - 1 (mod the tile axis's size); at most 4 entries of a list are owned by one tile index, and exactly 4 by t itself.
All inputs are finite; a program needn't handle non-finite values.
Results may differ from the reference program's by a relative error of at most 0.00064.
Values sent between devices are 32-bit elements; how exact they have to be, the bound alone decides.
No kernel may reach another device: no remote copies, remote signals or barrier semaphores. Data moves between devices by JAX's collectives and lax.ppermute only.
A program may use at most 128 MiB of HBM per device.

```python
import jax
import jax.numpy as jnp
from jax import lax

FEAT = 240
C1 = 64
C2 = 128
ROW = 128
BLK_DEV = 128
CTY_DEV = 12
SLOTS = 8
MOST = 4
REACH = 4
PIX_DEV = 16384
COUNTIES = 384
GRADS = 40256
N_STATE = 8
N_TILE = 32


def place_table(key):
    keys = jax.random.split(jax.random.fold_in(key, 11), N_STATE)
    return jax.vmap(lambda one: jax.random.permutation(one, COUNTIES))(keys).astype(jnp.int32)


def draw_county_place(key, part):
    return place_table(key)


def draw_tile_counties(key, part):
    table = place_table(key)
    inverse = jnp.argsort(table, axis=1).astype(jnp.int32)
    first, second, third = jax.random.split(jax.random.fold_in(key, 23), 3)
    far = jax.random.randint(first, (N_STATE, N_TILE, SLOTS - MOST), 1, REACH).astype(jnp.int32)
    offsets = jnp.concatenate([jnp.zeros((N_STATE, N_TILE, MOST), jnp.int32), far], axis=2)
    orders = jax.vmap(lambda one: jax.random.permutation(one, SLOTS))(jax.random.split(second, N_STATE * N_TILE))
    offsets = jnp.take_along_axis(offsets, orders.reshape(N_STATE, N_TILE, SLOTS).astype(jnp.int32), axis=2)
    same = offsets[..., :, None] == offsets[..., None, :]
    before = jnp.arange(SLOTS)[None, :] < jnp.arange(SLOTS)[:, None]
    rank = jnp.sum(same & before, axis=-1).astype(jnp.int32)
    starts = jax.random.randint(third, (N_STATE, N_TILE, REACH), 0, CTY_DEV).astype(jnp.int32)
    start = jnp.take_along_axis(starts, offsets, axis=2)
    owner = (jnp.arange(N_TILE, dtype=jnp.int32)[None, :, None] + offsets) % N_TILE
    place = owner * CTY_DEV + (start + rank) % CTY_DEV
    county = jnp.take_along_axis(inverse, place.reshape(N_STATE, N_TILE * SLOTS), axis=1)
    return county.astype(jnp.int32)


def draw_bands(key, part):
    first, second = jax.random.split(jax.random.fold_in(key, 31), 2)
    blocks = N_TILE * BLK_DEV
    base = jax.random.normal(first, (N_STATE, FEAT, blocks, 1), jnp.float32)
    noise = jax.random.normal(second, (N_STATE, FEAT, blocks, ROW), jnp.float32)
    values = 0.8 * base + 0.6 * noise
    return values.reshape(N_STATE, FEAT, blocks * ROW).astype(jnp.bfloat16)


def touch_ends(entries, rng, low, largest):
    shape = entries.shape
    index_at = [jax.random.randint(jax.random.fold_in(rng, axis), (), 0, shape[axis]) for axis in range(len(shape))]
    entries = entries.at[tuple(index_at)].set(low)
    longest = shape.index(max(shape))
    index_at[longest] = (index_at[longest] + 1) % shape[longest]
    return entries.at[tuple(index_at)].set(largest)


def centred(stream_key, dims, scale, most, kind=jnp.bfloat16):
    entries = scale * jax.random.normal(stream_key, dims, jnp.float32)
    return jnp.clip(entries, min=-most, max=most).astype(kind)


def setup_inputs(seed: int = 0) -> dict:
    key_of = jax.random.split(jax.random.key(seed), 11)
    bands = draw_bands(jax.random.fold_in(key_of[10], 71), 0)
    block_slot = touch_ends(jax.random.randint(key_of[1], (N_STATE, N_TILE * BLK_DEV), 0, SLOTS), jax.random.fold_in(key_of[1], 1), 0, SLOTS - 1).astype(jnp.int32)
    tile_counties = draw_tile_counties(jax.random.fold_in(key_of[10], 71), 0)
    county_place = draw_county_place(jax.random.fold_in(key_of[10], 71), 0)
    label = touch_ends(jax.random.randint(key_of[4], (N_STATE, COUNTIES), -200, 201), jax.random.fold_in(key_of[4], 1), -200, 200).astype(jnp.int32)
    w_first = centred(key_of[5], (C1, FEAT), FEAT ** -0.5, 0.375)
    taps = centred(key_of[6], (3, C1), 0.5, 2.0, jnp.float32)
    w_second = centred(key_of[7], (C2, C1), C1 ** -0.5, 0.75)
    w_third = centred(key_of[8], (C2, C2), C2 ** -0.5, 0.5)
    w_head = centred(key_of[9], (C2,), C2 ** -0.5, 0.5)
    return {"bands": bands, "block_slot": block_slot, "tile_counties": tile_counties, "county_place": county_place, "label": label, "w_first": w_first, "taps": taps, "w_second": w_second, "w_third": w_third, "w_head": w_head}


def silu_parts(value):
    sig = jax.nn.sigmoid(value)
    return value * sig, sig * (1.0 + value * (1.0 - sig))


def along_rows(field, weights, row_len):
    chans, count = field.shape
    grid = field.reshape(chans, count // row_len, row_len)
    padded = jnp.pad(grid, ((0, 0), (0, 0), (1, 1)))
    out = weights[0][:, None, None] * padded[:, :, :-2] + weights[1][:, None, None] * grid + weights[2][:, None, None] * padded[:, :, 2:]
    return out.reshape(chans, count)


def tap_grads(field, upstream, row_len):
    chans, count = field.shape
    grid = field.reshape(chans, count // row_len, row_len)
    padded = jnp.pad(grid, ((0, 0), (0, 0), (1, 1)))
    above = upstream.reshape(grid.shape)
    return jnp.stack([jnp.sum(above * padded[:, :, :-2], axis=(1, 2)), jnp.sum(above * grid, axis=(1, 2)), jnp.sum(above * padded[:, :, 2:], axis=(1, 2))])


def contract_last(left, right):
    return lax.dot_general(left, right, (((1,), (1,)), ((), ())), preferred_element_type=jnp.float32)


def contract_first(left, right):
    return lax.dot_general(left, right, (((0,), (0,)), ((), ())), preferred_element_type=jnp.float32)


def forward(pixels, w_first, taps, w_second, w_third, w_head, row_len):
    h_one = jnp.dot(w_first, pixels, preferred_element_type=jnp.float32)
    s_one = along_rows(h_one, taps, row_len)
    a_one = silu_parts(s_one)[0].astype(jnp.bfloat16)
    h_two = jnp.dot(w_second, a_one, preferred_element_type=jnp.float32)
    a_two = silu_parts(h_two)[0].astype(jnp.bfloat16)
    h_three = jnp.dot(w_third, a_two, preferred_element_type=jnp.float32)
    a_three = (silu_parts(h_three)[0] + a_two.astype(jnp.float32)).astype(jnp.bfloat16)
    yhat = jnp.dot(w_head, a_three, preferred_element_type=jnp.float32)
    return h_one, s_one, a_one, h_two, a_two, h_three, a_three, yhat


def backward(pixels, saved, w_first, taps, w_second, w_third, w_head, cotangent, row_len):
    h_one, s_one, a_one, h_two, a_two, h_three, a_three, yhat = saved
    grad_in = cotangent.astype(jnp.bfloat16)
    d_head = jnp.dot(a_three, grad_in, preferred_element_type=jnp.float32)
    d_a3 = w_head.astype(jnp.float32)[:, None] * grad_in.astype(jnp.float32)[None, :]
    d_h3 = (d_a3 * silu_parts(h_three)[1]).astype(jnp.bfloat16)
    d_third = contract_last(d_h3, a_two)
    d_a2 = contract_first(w_third, d_h3) + d_a3
    d_h2 = (d_a2 * silu_parts(h_two)[1]).astype(jnp.bfloat16)
    d_second = contract_last(d_h2, a_one)
    d_a1 = contract_first(w_second, d_h2)
    d_s1 = d_a1 * silu_parts(s_one)[1]
    d_taps = tap_grads(h_one, d_s1, row_len)
    d_h1 = along_rows(d_s1, jnp.stack([taps[2], taps[1], taps[0]]), row_len).astype(jnp.bfloat16)
    d_first = contract_last(d_h1, pixels)
    return jnp.concatenate([d_first.reshape(-1), d_taps.reshape(-1), d_second.reshape(-1), d_third.reshape(-1), d_head])


def slot_stats(yhat, slots, slot_count):
    blocks = slots.shape[0]
    row_len = yhat.shape[0] // blocks
    member = (slots[None, :] == jnp.arange(slot_count, dtype=jnp.int32)[:, None]).astype(jnp.float32)
    block_sums = jnp.sum(yhat.reshape(blocks, row_len), axis=1)
    return jnp.sum(member * block_sums[None, :], axis=1), jnp.sum(member, axis=1) * row_len, member


def place_of(counties, table):
    hits = counties[:, None] == jnp.arange(table.shape[0], dtype=jnp.int32)[None, :]
    return jnp.sum(jnp.where(hits, table[None, :], 0), axis=1).astype(jnp.int32)


def judge(sums, counts, labels, devices):
    denom = jnp.maximum(counts, 1.0)
    mean = sums / denom
    live = (counts > 0.5).astype(jnp.float32)
    target = labels.astype(jnp.float32) * 0.01
    return mean, live * 2.0 * (mean - target) / (devices * denom)


def pixel_cotangent(member, slot_adjoint, row_len):
    block_adjoint = jnp.sum(member * slot_adjoint[:, None], axis=0)
    return jnp.broadcast_to(block_adjoint[:, None], (block_adjoint.shape[0], row_len)).reshape(-1)


def reference(bands, block_slot, tile_counties, county_place, label, w_first, taps, w_second, w_third, w_head):
    n_dev = N_STATE * N_TILE
    county_iota = jnp.arange(COUNTIES, dtype=jnp.int32)
    state_iota = jnp.arange(N_STATE, dtype=jnp.int32)

    def device_slice(index):
        state = (index // N_TILE).astype(jnp.int32)
        tile = (index % N_TILE).astype(jnp.int32)
        zero = jnp.zeros((), jnp.int32)
        pixels = lax.dynamic_slice(bands, (state, zero, tile * PIX_DEV), (1, FEAT, PIX_DEV))[0]
        slots = lax.dynamic_slice(block_slot, (state, tile * BLK_DEV), (1, BLK_DEV))[0]
        counties = lax.dynamic_slice(tile_counties, (state, tile * SLOTS), (1, SLOTS))[0]
        table = lax.dynamic_slice(county_place, (state, zero), (1, COUNTIES))[0]
        return state, pixels, slots, counties, table

    def first_pass(carry, index):
        sums, counts = carry
        state, pixels, slots, counties, table = device_slice(index)
        yhat = forward(pixels, w_first, taps, w_second, w_third, w_head, ROW)[-1]
        slot_sums, slot_counts, member = slot_stats(yhat, slots, SLOTS)
        hit = (place_of(counties, table)[:, None] == county_iota[None, :]).astype(jnp.float32)
        row = (state_iota == state).astype(jnp.float32)[:, None]
        sums = sums + row * jnp.sum(hit * slot_sums[:, None], axis=0)[None, :]
        counts = counts + row * jnp.sum(hit * slot_counts[:, None], axis=0)[None, :]
        return (sums, counts), None

    zeros = jnp.zeros((N_STATE, COUNTIES), jnp.float32)
    (sums, counts), _ = lax.scan(first_pass, (zeros, zeros), jnp.arange(n_dev, dtype=jnp.int32))
    county_mean, adjoint = judge(sums, counts, label, float(n_dev))

    def second_pass(total, index):
        state, pixels, slots, counties, table = device_slice(index)
        saved = forward(pixels, w_first, taps, w_second, w_third, w_head, ROW)
        member = slot_stats(saved[-1], slots, SLOTS)[2]
        hit = (place_of(counties, table)[:, None] == county_iota[None, :]).astype(jnp.float32)
        row = jnp.sum((state_iota == state).astype(jnp.float32)[:, None] * adjoint, axis=0)
        slot_adjoint = jnp.sum(hit * row[None, :], axis=1)
        cotangent = pixel_cotangent(member, slot_adjoint, ROW)
        return total + backward(pixels, saved, w_first, taps, w_second, w_third, w_head, cotangent, ROW), None

    weight_grads, _ = lax.scan(second_pass, jnp.zeros((GRADS,), jnp.float32), jnp.arange(n_dev, dtype=jnp.int32))
    return county_mean, weight_grads
```

```python
import functools

import jax
import jax.numpy as jnp
from jax import lax
from jax.experimental import pallas as pl
from jax.experimental.pallas import tpu as pltpu
from jax.sharding import Mesh
from jax.sharding import PartitionSpec as P

MOST = 4
REACH = 4
ROW = 128
SLOTS = 8
PIECES = 32
PIECE = 1280
F32 = jnp.float32
BF16 = jnp.bfloat16
TILE = ("x", "y", "core")


def mm(left, right):
    return jnp.dot(left, right, preferred_element_type=F32)


def mm_nt(left, right):
    return lax.dot_general(left, right, (((1,), (1,)), ((), ())), preferred_element_type=F32)


def roll_rows(field, by):
    count = field.shape[1] // ROW
    parts = [pltpu.roll(field[:, i * ROW : (i + 1) * ROW], by % ROW, 1) for i in range(count)]
    return parts[0] if count == 1 else jnp.concatenate(parts, axis=1)


def wide(field, count):
    return field if count == 1 else jnp.concatenate([field] * count, axis=1)


def gate(value):
    half = 0.5 * value
    turn = jnp.tanh(half)
    plus = 1.0 + turn
    out = half * plus
    return out, 0.5 * (plus + out * (1.0 - turn))


def forward_kernel(
    slots, x_ref, w1, tapm, w2, w3, whb, a1_ref, q1_ref, a2_ref, q2_ref, d3_ref, heads_ref, sums
):
    step = pl.program_id(0)

    @pl.when(step == 0)
    def _():
        sums[...] = jnp.zeros_like(sums)

    px = x_ref.shape[1]
    n = 2
    for c in range(px // (n * ROW)):
        at = pl.ds(c * n * ROW, n * ROW)
        h1 = mm(w1[...], x_ref[:, at])
        s1 = wide(tapm[0], n) * roll_rows(h1, 1) + wide(tapm[1], n) * h1
        s1 = s1 + wide(tapm[2], n) * roll_rows(h1, -1)
        a1, q1 = gate(s1)
        a1 = a1.astype(BF16)
        a1_ref[:, at] = a1
        q1_ref[:, at] = q1.astype(BF16)
        a2, q2 = gate(mm(w2[...], a1))
        a2 = a2.astype(BF16)
        a2_ref[:, at] = a2
        q2_ref[:, at] = q2.astype(BF16)
        a3, q3 = gate(mm(w3[...], a2))
        d3_ref[:, at] = (wide(whb[...], n) * q3).astype(BF16)
        a3 = (a3 + a2.astype(F32)).astype(BF16).astype(F32)
        for j in range(n):
            slot = slots[step * (px // ROW) + c * n + j]
            sums[slot] += a3[:, j * ROW : (j + 1) * ROW]

    @pl.when(step == pl.num_programs(0) - 1)
    def _():
        for s in range(SLOTS):
            heads_ref[s : s + 1, :] = jnp.sum(jnp.transpose(sums[s]), axis=0, keepdims=True)


def whole(shape):
    zeros = (0,) * len(shape)
    return pl.BlockSpec(shape, lambda i, s: zeros)


def forward(slots, pixels, w1, tapm, w2, w3, whb, px=1024):
    total = pixels.shape[1]
    c1, c2 = w2.shape[1], w2.shape[0]
    chans = [c1, c1, c2, c2, c2]
    cols = lambda ch: pl.BlockSpec((ch, px), lambda i, s: (0, i))
    consts = (w1, tapm, w2, w3, whb)
    return pl.pallas_call(
        forward_kernel,
        out_shape=[jax.ShapeDtypeStruct((ch, total), BF16) for ch in chans]
        + [jax.ShapeDtypeStruct((SLOTS, c2), F32)],
        grid_spec=pltpu.PrefetchScalarGridSpec(
            num_scalar_prefetch=1,
            grid=(total // px,),
            in_specs=[cols(pixels.shape[0])] + [whole(w.shape) for w in consts],
            out_specs=[cols(ch) for ch in chans] + [whole((SLOTS, c2))],
            scratch_shapes=[pltpu.VMEM((SLOTS, c2, ROW), F32)],
        ),
        compiler_params=pltpu.CompilerParams(dimension_semantics=("arbitrary",)),
        cost_estimate=pl.CostEstimate(
            flops=2 * total * 40000, bytes_accessed=25_000_000, transcendentals=total * 320
        ),
        name="forward",
    )(slots, pixels, *consts)


def backward_kernel(first, carry, *refs):
    slots, x_ref, a1_ref, q1_ref, a2_ref, q2_ref, d3_ref, w2t, w3t, whb, edge = refs[:11]
    g1_ref, g2_ref, g3_ref = refs[-3:]
    step = pl.program_id(0)

    @pl.when(step == 0)
    def _():
        for i, ref in enumerate((g1_ref, g2_ref, g3_ref)):
            ref[...] = refs[11 + i][...] if carry else jnp.zeros_like(ref)

    px = x_ref.shape[1]
    n = 2
    for c in range(px // (n * ROW)):
        at = pl.ds(c * n * ROW, n * ROW)
        d3 = d3_ref[:, at]
        da2 = mm(w3t[...], d3) + wide(whb[...], n)
        dh2 = (da2 * q2_ref[:, at].astype(F32)).astype(BF16)
        ds = mm(w2t[...], dh2) * q1_ref[:, at].astype(F32)
        after = (roll_rows(ds, -1) * wide(edge[1], n)).astype(BF16)
        before = (roll_rows(ds, 1) * wide(edge[0], n)).astype(BF16)
        stack = jnp.concatenate([after, ds.astype(BF16), before], axis=0)
        for j in range(n):
            slot = slots[(first + step) * (px // ROW) + c * n + j]
            o = slice(j * ROW, (j + 1) * ROW)
            r = pl.ds((c * n + j) * ROW, ROW)
            g3_ref[slot] += mm_nt(d3[:, o], a2_ref[:, r])
            g2_ref[slot] += mm_nt(dh2[:, o], a1_ref[:, r])
            g1_ref[slot] += mm_nt(stack[:, o], x_ref[:, r])


def backward(first, blocks, slots, pixels, saved, consts, start=None, px=1024):
    a1, q1, a2, q2, d3 = saved
    ft, c1, c2 = pixels.shape[0], a1.shape[0], a2.shape[0]
    cols = lambda ch: pl.BlockSpec((ch, px), lambda i, s: (0, first + i))
    outs = [(SLOTS, 3 * c1, ft), (SLOTS, c2, c1), (SLOTS, c2, c2)]
    extra = () if start is None else tuple(start)
    return pl.pallas_call(
        functools.partial(backward_kernel, first, start is not None),
        out_shape=[jax.ShapeDtypeStruct(s, F32) for s in outs],
        grid_spec=pltpu.PrefetchScalarGridSpec(
            num_scalar_prefetch=1,
            grid=(blocks,),
            in_specs=[cols(v.shape[0]) for v in (pixels, a1, q1, a2, q2, d3)]
            + [whole(w.shape) for w in consts + extra],
            out_specs=[whole(s) for s in outs],
        ),
        compiler_params=pltpu.CompilerParams(dimension_semantics=("arbitrary",)),
        cost_estimate=pl.CostEstimate(
            flops=2 * blocks * px * 64000, bytes_accessed=blocks * 1_500_000, transcendentals=0
        ),
        name="backward",
    )(slots, pixels, a1, q1, a2, q2, d3, *consts, *extra)


def combine_kernel(coef, g1_ref, g2_ref, g3_ref, heads_ref, w1, tapc, out_ref, lo, hi, rows):
    c1 = w1.shape[0]
    ft = w1.shape[1]

    def mixed(ref):
        total = coef[0] * ref[0]
        for s in range(1, SLOTS):
            total = total + coef[s] * ref[s]
        return total

    parts = mixed(g1_ref)
    after, same, before = parts[:c1], parts[c1 : 2 * c1], parts[2 * c1 :]
    first = tapc[:, 0:1] * after + tapc[:, 1:2] * same + tapc[:, 2:3] * before
    lo[0:c1, :] = first[:, :ROW]
    hi[...] = jnp.zeros_like(hi)
    hi[:, 0 : ft - ROW] = first[:, ROW:]
    filled = 15

    def near_row(src):
        at = pl.ds(src, 8, stride=8)
        return jnp.concatenate([lo[at, :], hi[at, :]], axis=1)

    lane = lax.broadcasted_iota(jnp.int32, (8, ROW), 1)
    for p in range(filled):
        src, at = divmod(p * ROW, ft)
        near = near_row(src)
        piece = pltpu.roll(near, (-at) % 256, 1)[:, :ROW] if at else near[:, :ROW]
        left = ft - at
        if left < ROW:
            far = lo[pl.ds(src + 1, 8, stride=8), :]
            piece = jnp.where(lane < left, piece, pltpu.roll(far, left, 1))
        rows[pl.ds(p, 8, stride=filled), :] = piece
    base = c1 * ft // ROW
    wf = w1[...].astype(F32)
    half = ROW // 2
    tap_rows = []
    for part in (after, same, before):
        tap_rows.append(jnp.sum(jnp.transpose(wf * part), axis=0, keepdims=True))
    second = mixed(g2_ref)
    third = mixed(g3_ref)
    head = coef[0] * heads_ref[0:1, :]
    for s in range(1, SLOTS):
        head = head + coef[s] * heads_ref[s : s + 1, :]
    c2 = second.shape[0]
    rows[base : base + 1, :] = jnp.concatenate([tap_rows[0], tap_rows[1]], axis=1)
    lo[:, 0:half] = second
    even = lo[pl.ds(0, c2 // 2, stride=2), :]
    odd = lo[pl.ds(1, c2 // 2, stride=2), :]
    low = lax.broadcasted_iota(jnp.int32, (c2 // 2, ROW), 1) < half
    rows[base + 2 : base + 1 + c2 // 2, :] = jnp.where(
        low[: c2 // 2 - 1], odd[: c2 // 2 - 1], pltpu.roll(even, half, 1)[1:]
    )
    rows[base + 1 : base + 2, :] = jnp.concatenate([tap_rows[2], second[0:1]], axis=1)
    mark = base + 1 + c2 // 2
    turned = pltpu.roll(third, half, 1)
    rows[mark : mark + 1, :] = jnp.where(low[0:1], odd[c2 // 2 - 1 :], turned[0:1])
    low = lax.broadcasted_iota(jnp.int32, (c2, ROW), 1) < half
    rows[mark + 1 : mark + c2, :] = jnp.where(low[1:], turned[: c2 - 1], turned[1:])
    turned_head = pltpu.roll(head, half, 1)
    rows[mark + c2 : mark + c2 + 1, :] = jnp.where(low[0:1], turned[c2 - 1 :], turned_head)
    rows[mark + c2 + 1 : mark + c2 + 2, :] = jnp.where(low[0:1], turned_head, 0.0)
    rest = rows.shape[0] - (mark + c2 + 2)
    rows[mark + c2 + 2 :, :] = jnp.zeros((rest, ROW), F32)
    each = PIECE // ROW
    for j in range(each):
        out_ref[:, j * ROW : (j + 1) * ROW] = rows[pl.ds(j, PIECES, stride=each), :]


def combine(coef, grads, heads, w1, tapc):
    args = (*grads, heads, w1, tapc)
    return pl.pallas_call(
        combine_kernel,
        out_shape=jax.ShapeDtypeStruct((PIECES, PIECE), F32),
        grid_spec=pltpu.PrefetchScalarGridSpec(
            num_scalar_prefetch=1,
            grid=(1,),
            in_specs=[whole(a.shape) for a in args],
            out_specs=whole((PIECES, PIECE)),
            scratch_shapes=[
                pltpu.VMEM((2 * w1.shape[0], ROW), F32),
                pltpu.VMEM((w1.shape[0], ROW), F32),
                pltpu.VMEM((PIECES * PIECE // ROW, ROW), F32),
            ],
        ),
        name="combine",
    )(coef, *args)


def from_behind(value, by):
    sizes = [lax.axis_size(a) for a in TILE]
    peers = sizes[0] * sizes[1] * sizes[2]
    return lax.ppermute(value, TILE, [(i, (i + by) % peers) for i in range(peers)])


def place_of(counties, table):
    hits = counties[:, None] == jnp.arange(table.shape[0], dtype=jnp.int32)[None, :]
    return jnp.sum(jnp.where(hits, table[None, :], 0), axis=1)


def judge(sums, counts, labels, devices):
    denom = jnp.maximum(counts, 1.0)
    mean = sums / denom
    live = (counts > 0.5).astype(F32)
    target = labels.astype(F32) * 0.01
    return mean, live * 2.0 * (mean - target) / (devices * denom)


def settle(sums, counts, codes, labels, devices):
    owned = jnp.arange(1, labels.shape[0] + 1, dtype=jnp.int32).astype(F32)
    hit = (codes[:, None] == owned[None, :]).astype(F32)
    total = jnp.sum(hit * sums[:, None], axis=0)
    number = jnp.sum(hit * counts[:, None], axis=0)
    mean, adjoint = judge(total, number, labels, devices)
    return mean, jnp.sum(hit * adjoint[None, :], axis=1)


def swap(value, axes):
    return lax.all_to_all(value, axes, 0, 0, tiled=True)


def summed_everywhere(pieces):
    mine = jnp.sum(swap(pieces, TILE), axis=0)
    states = lax.axis_size("z")
    mine = jnp.sum(swap(jnp.broadcast_to(mine[None], (states, PIECE)), ("z",)), axis=0)
    return swap(jnp.broadcast_to(mine[None], (PIECES, PIECE)), TILE)


def on_device(
    bands, block_slot, tile_counties, county_place, label, w_first, taps, w_second, w_third, w_head
):
    pixels = bands[0]
    slots = block_slot[0]
    labels_mine = label[0]
    cty_dev = labels_mine.shape[0]
    n_tile = PIECES
    devices = float(lax.axis_size("z") * n_tile)
    lane = jnp.arange(ROW)
    edge = jnp.stack([lane > 0, lane < ROW - 1]).astype(F32)
    c1, c2 = w_second.shape[1], w_second.shape[0]
    edge = jnp.broadcast_to(edge[:, None, :], (2, c1, ROW))
    tapm = taps[:, :, None] * jnp.stack([edge[0], jnp.ones_like(edge[0]), edge[1]])
    whf = w_head.astype(F32)
    whb = jnp.broadcast_to(whf[:, None], (c2, ROW))
    *saved, heads = forward(slots, pixels, w_first, tapm, w_second, w_third, whb)

    member = (slots[None, :] == jnp.arange(SLOTS, dtype=jnp.int32)[:, None]).astype(F32)
    slot_counts = jnp.sum(member, axis=1) * float(ROW)
    place = place_of(tile_counties[0], county_place[0])
    owner = place // cty_dev
    local_code = (place % cty_dev + 1).astype(F32)
    order = jnp.arange(SLOTS, dtype=jnp.int32)
    rank = jnp.sum(
        ((owner[:, None] == owner[None, :]) & (order[None, :] < order[:, None])).astype(jnp.int32),
        axis=1,
    )
    me = (lax.axis_index("x") * 4 + lax.axis_index("y")) * 2 + lax.axis_index("core")
    position = (owner - me) % n_tile * MOST + rank
    select = (position[:, None] == jnp.arange(REACH * MOST, dtype=jnp.int32)[None, :]).astype(F32)

    slot_sums = jnp.sum(heads * whf[None, :], axis=1)
    values = jnp.stack([slot_sums, slot_counts, local_code])
    out = jnp.sum(values[:, :, None] * select[None], axis=1).reshape(3, REACH, MOST)
    got = [out[:, 0]] + [from_behind(out[:, step], step) for step in range(1, REACH)]
    got = jnp.stack(got, axis=1).reshape(3, REACH * MOST)
    county_mean, back = settle(got[0], got[1], got[2], labels_mine, devices)
    back = back.reshape(REACH, MOST)
    home = [back[0]] + [from_behind(back[step], -step) for step in range(1, REACH)]
    slot_adjoint = jnp.sum(select * jnp.stack(home).reshape(1, -1), axis=1)
    coef = slot_adjoint.astype(BF16).astype(F32)

    consts = (w_second.T, w_third.T, whb, edge)
    grads = backward(0, 16, slots, pixels, saved, consts)
    pieces = combine(coef, grads, heads, w_first, taps.T)
    total = summed_everywhere(pieces)
    count = w_first.size + taps.size + w_second.size + w_third.size + w_head.size
    return county_mean[None, :], total.reshape(-1)[:count]


def solution(mesh):
    shape = mesh.devices.shape
    fine = Mesh(mesh.devices.reshape(shape[0], 4, 4, 2), ("z",) + TILE)
    in_specs = (
        P("z", None, TILE),
        P("z", TILE),
        P("z", TILE),
        P("z", None),
        P("z", TILE),
        P(),
        P(),
        P(),
        P(),
        P(),
    )
    return jax.shard_map(
        on_device, mesh=fine, in_specs=in_specs, out_specs=(P("z", TILE), P()), check_vma=False
    )
```

```python
import functools

import jax
import jax.numpy as jnp
from jax import lax
from jax.experimental import pallas as pl
from jax.experimental.pallas import tpu as pltpu
from jax.sharding import Mesh
from jax.sharding import PartitionSpec as P

MOST = 4
REACH = 4
ROW = 128
SLOTS = 8
PIECES = 32
PIECE = 1280
F32 = jnp.float32
BF16 = jnp.bfloat16
TILE = ("x", "y", "core")
STEP_PX = 1024


def mm(left, right):
    return jnp.dot(left, right, preferred_element_type=F32)


def mm_nt(left, right):
    return lax.dot_general(left, right, (((1,), (1,)), ((), ())), preferred_element_type=F32)


def iota(shape, axis):
    return lax.broadcasted_iota(jnp.int32, shape, axis)


def as_column(row, count):
    square = iota((count, count), 0) == iota((count, count), 1)
    return jnp.sum(jnp.where(square, row, 0.0), axis=1, keepdims=True)


def roll_rows(field, by):
    count = field.shape[1] // ROW
    parts = [pltpu.roll(field[:, i * ROW : (i + 1) * ROW], by % ROW, 1) for i in range(count)]
    return parts[0] if count == 1 else jnp.concatenate(parts, axis=1)


def wide(field, count):
    return field if count == 1 else jnp.concatenate([field] * count, axis=1)


def gate(half):
    plus = 1.0 + jnp.tanh(half)
    out = half * plus
    low, plus = out.astype(BF16), plus.astype(BF16)
    return out, low, plus + low * (2.0 - plus)


def whole(shape):
    zeros = (0,) * len(shape)
    return pl.BlockSpec(shape, lambda i, *s: zeros)


def slot_positions(counties, table, me, cty_dev):
    owners, codes, positions = [], [], []
    for s in range(SLOTS):
        place = table[counties[s]]
        owner = lax.div(place, cty_dev)
        rank = jnp.int32(0)
        for other in owners:
            rank = rank + (other == owner).astype(jnp.int32)
        owners.append(owner)
        codes.append(place - owner * cty_dev + 1)
        positions.append(lax.rem(owner - me[0] + PIECES, PIECES) * MOST + rank)
    return positions, codes


def forward_kernel(
    cty_dev, slots, counties, table, me,
    x_ref, slotv, w1, taps, w2t, w3, wh,
    a1_ref, a2_ref, d3_ref, dh2_ref, ds_ref, heads_ref, s0, s1_, s2_, s3_,
    tapm, w2h, w3h, w2th, w3th, whb, whf, acc,
):
    step = pl.program_id(0)
    c2, c1 = w3.shape[0], w2t.shape[0]
    n = 2

    @pl.when(step == 0)
    def _():
        lane = iota((c1, ROW), 1)
        for k in range(3):
            col = jnp.broadcast_to(0.5 * as_column(taps[k : k + 1, :], c1), (c1, ROW))
            if k == 0:
                col = jnp.where(lane > 0, col, 0.0)
            if k == 2:
                col = jnp.where(lane < ROW - 1, col, 0.0)
            tapm[k] = col
        half2t = 0.5 * w2t[...].astype(F32)
        half3 = 0.5 * w3[...].astype(F32)
        w2th[...] = half2t.astype(BF16)
        w2h[...] = jnp.transpose(half2t).astype(BF16)
        w3h[...] = half3.astype(BF16)
        w3th[...] = jnp.transpose(half3).astype(BF16)
        col = jnp.broadcast_to(0.5 * as_column(wh[...].astype(F32), c2), (c2, ROW))
        whf[...] = col
        whb[...] = col.astype(BF16)
        acc[...] = jnp.zeros_like(acc)

    px = x_ref.shape[1]
    heads = jnp.zeros(acc.shape, F32)
    for c in range(px // (n * ROW)):
        at = pl.ds(c * n * ROW, n * ROW)
        h1 = mm(w1[...], x_ref[:, at])
        s1 = wide(tapm[0], n) * roll_rows(h1, 1) + wide(tapm[1], n) * h1
        s1 = s1 + wide(tapm[2], n) * roll_rows(h1, -1)
        _, a1, q1 = gate(s1)
        a1_ref[:, at] = a1
        _, a2, q2 = gate(mm(w2h[...], a1))
        a2_ref[:, at] = a2
        out, _, q3 = gate(mm(w3h[...], a2))
        a3 = (out + a2.astype(F32)).astype(BF16)
        d3 = wide(whb[...], n) * q3
        d3_ref[:, at] = d3
        member = []
        for j in range(n):
            slot = slots[step * (px // ROW) + c * n + j]
            member.append((iota(acc.shape, 0) == slot).astype(F32).astype(BF16))
        heads = heads + mm_nt(jnp.concatenate(member, axis=1), a3)
        dh2 = (mm(w3th[...], d3) + wide(whf[...], n)).astype(BF16) * q2
        dh2_ref[:, at] = dh2
        ds_ref[:, at] = mm(w2th[...], dh2).astype(BF16) * q1
    acc[...] += heads

    @pl.when(step == pl.num_programs(0) - 1)
    def _():
        per_slot = acc[0:SLOTS, :]
        heads_ref[...] = per_slot
        sums = jnp.sum(per_slot * wh[...].astype(F32), axis=1, keepdims=True)
        counts = (slotv[...] == iota((SLOTS, slotv.shape[1]), 0)).astype(F32)
        counts = jnp.sum(counts, axis=1, keepdims=True) * float(ROW)
        positions, codes = slot_positions(counties, table, me, cty_dev)
        lane = iota((SLOTS, ROW), 1)
        row = iota((SLOTS, ROW), 0)
        packed = jnp.zeros((SLOTS, ROW), F32)
        for s in range(SLOTS):
            value = jnp.where(row == 0, sums[s : s + 1, :], counts[s : s + 1, :])
            value = jnp.where(row == 2, codes[s].astype(F32), value)
            packed = jnp.where(lane == positions[s], value, packed)
        for k, ref in enumerate((s0, s1_, s2_, s3_)):
            ref[...] = pltpu.roll(packed, (-MOST * k) % ROW, 1)


def forward(cty_dev, scalars, slotv, pixels, w1, taps, w2t, w3, wh):
    total = pixels.shape[1]
    c1, c2 = w2t.shape[0], w2t.shape[1]
    chans = [c1, c2, c2, c2, c1]
    px = STEP_PX
    cols = lambda ch: pl.BlockSpec((ch, px), lambda i, *s: (0, i))
    consts = (slotv, w1, taps, w2t, w3, wh)
    small = [(SLOTS, c2)] + [(SLOTS, ROW)] * REACH
    return pl.pallas_call(
        functools.partial(forward_kernel, cty_dev),
        out_shape=[jax.ShapeDtypeStruct((ch, total), BF16) for ch in chans]
        + [jax.ShapeDtypeStruct(s, F32) for s in small],
        grid_spec=pltpu.PrefetchScalarGridSpec(
            num_scalar_prefetch=4,
            grid=(total // px,),
            in_specs=[cols(pixels.shape[0])] + [whole(w.shape) for w in consts],
            out_specs=[cols(ch) for ch in chans] + [whole(s) for s in small],
            scratch_shapes=[
                pltpu.VMEM((3, c1, ROW), F32),
                pltpu.VMEM((c2, c1), BF16),
                pltpu.VMEM((c2, c2), BF16),
                pltpu.VMEM((c1, c2), BF16),
                pltpu.VMEM((c2, c2), BF16),
                pltpu.VMEM((c2, ROW), BF16),
                pltpu.VMEM((c2, ROW), F32),
                pltpu.VMEM((16, c2), F32),
            ],
        ),
        compiler_params=pltpu.CompilerParams(dimension_semantics=("arbitrary",)),
        cost_estimate=pl.CostEstimate(
            flops=2 * total * 75000, bytes_accessed=25_000_000, transcendentals=total * 320
        ),
        name="forward",
    )(*scalars, pixels, *consts)


def settle_kernel(devices, cty_dev, p0, p1, p2, p3, label, mean_ref, b0, b1, b2, b3):
    size = 16
    lane = iota((SLOTS, ROW), 1)
    got = jnp.zeros((SLOTS, ROW), F32)
    for k, ref in enumerate((p0, p1, p2, p3)):
        moved = pltpu.roll(ref[...], MOST * k, 1) if k else ref[...]
        got = jnp.where((lane >= MOST * k) & (lane < MOST * (k + 1)), moved, got)
    owned = iota((size, ROW), 0)
    hit = (got[2:3, :] == (owned + 1).astype(F32)) & (owned < cty_dev)
    total = jnp.sum(jnp.where(hit, got[0:1, :], 0.0), axis=1, keepdims=True)
    number = jnp.sum(jnp.where(hit, got[1:2, :], 0.0), axis=1, keepdims=True)
    same = owned == iota((size, ROW), 1)
    labels = jnp.concatenate(
        [label[...].astype(F32), jnp.zeros((1, ROW - label.shape[1]), F32)], axis=1
    )
    target = jnp.sum(jnp.where(same, labels, 0.0), axis=1, keepdims=True) * 0.01
    denom = jnp.maximum(number, 1.0)
    mean = total / denom
    live = jnp.where(number > 0.5, 2.0, 0.0)
    adjoint = live * (mean - target) / (devices * denom)
    spread = jnp.sum(jnp.where(same, mean, 0.0), axis=0, keepdims=True)
    mean_ref[...] = spread[:, :cty_dev]
    back = jnp.sum(jnp.where(hit, adjoint, 0.0), axis=0, keepdims=True)
    back = jnp.broadcast_to(back, (SLOTS, ROW))
    for k, ref in enumerate((b0, b1, b2, b3)):
        ref[...] = pltpu.roll(back, (-MOST * k) % ROW, 1)


def settle(devices, pieces, label):
    cty_dev = label.shape[1]
    tile = jax.ShapeDtypeStruct((SLOTS, ROW), F32)
    return pl.pallas_call(
        functools.partial(settle_kernel, devices, cty_dev),
        out_shape=[jax.ShapeDtypeStruct((1, cty_dev), F32)] + [tile] * REACH,
        name="settle",
    )(*pieces, label)


def write_flat(after, same, before, second, third, head, w1, taps, lo, hi, rows):
    c1, ft = w1.shape
    cols = [as_column(taps[k : k + 1, :], c1) for k in range(3)]
    first = cols[0] * after + cols[1] * same + cols[2] * before
    lo[0:c1, :] = first[:, :ROW]
    hi[...] = jnp.zeros_like(hi)
    hi[:, 0 : ft - ROW] = first[:, ROW:]
    filled = 15
    lane = iota((8, ROW), 1)
    for p in range(filled):
        src, at = divmod(p * ROW, ft)
        near = pl.ds(src, 8, stride=8)
        piece = jnp.concatenate([lo[near, :], hi[near, :]], axis=1)
        piece = pltpu.roll(piece, (-at) % 256, 1)[:, :ROW] if at else piece[:, :ROW]
        left = ft - at
        if left < ROW:
            far = lo[pl.ds(src + 1, 8, stride=8), :]
            piece = jnp.where(lane < left, piece, pltpu.roll(far, left, 1))
        rows[pl.ds(p, 8, stride=filled), :] = piece
    base = c1 * ft // ROW
    half = ROW // 2
    wf = w1[...].astype(F32)
    t0, t1, t2 = [
        jnp.sum(jnp.transpose(wf * part), axis=0, keepdims=True) for part in (after, same, before)
    ]
    c2 = second.shape[0]
    rows[base : base + 1, :] = jnp.concatenate([t0, t1], axis=1)
    lo[:, 0:half] = second
    even = lo[pl.ds(0, c2 // 2, stride=2), :]
    odd = lo[pl.ds(1, c2 // 2, stride=2), :]
    low = iota((c2, ROW), 1) < half
    rows[base + 2 : base + 1 + c2 // 2, :] = jnp.where(
        low[: c2 // 2 - 1], odd[: c2 // 2 - 1], pltpu.roll(even, half, 1)[1:]
    )
    rows[base + 1 : base + 2, :] = jnp.concatenate([t2, second[0:1]], axis=1)
    mark = base + 1 + c2 // 2
    turned = pltpu.roll(third, half, 1)
    rows[mark : mark + 1, :] = jnp.where(low[0:1], odd[c2 // 2 - 1 :], turned[0:1])
    rows[mark + 1 : mark + c2, :] = jnp.where(low[1:], turned[: c2 - 1], turned[1:])
    turned_head = pltpu.roll(head, half, 1)
    rows[mark + c2 : mark + c2 + 1, :] = jnp.where(low[0:1], turned[c2 - 1 :], turned_head)
    rows[mark + c2 + 1 : mark + c2 + 2, :] = jnp.where(low[0:1], turned_head, 0.0)
    rest = rows.shape[0] - (mark + c2 + 2)
    rows[mark + c2 + 2 :, :] = jnp.zeros((rest, ROW), F32)


def backward_kernel(
    cty_dev, slots, counties, table, me,
    x_ref, a1_ref, a2_ref, d3_ref, dh2_ref, ds_ref, heads, r0, r1, r2, r3, w1, taps,
    rows, g1, g2, g3, gtab, lo, hi,
):
    step = pl.program_id(0)
    c1 = a1_ref.shape[0]
    px = x_ref.shape[1]
    n = 4

    @pl.when(step == 0)
    def _():
        lane = iota((SLOTS, ROW), 1)
        back = jnp.zeros((SLOTS, ROW), F32)
        for k, ref in enumerate((r0, r1, r2, r3)):
            moved = pltpu.roll(ref[...], MOST * k, 1) if k else ref[...]
            back = jnp.where((lane >= MOST * k) & (lane < MOST * (k + 1)), moved, back)
        positions, _ = slot_positions(counties, table, me, cty_dev)
        row = iota((SLOTS, ROW), 0)
        spot = jnp.zeros((SLOTS, ROW), jnp.int32)
        for s in range(SLOTS):
            spot = jnp.where(row == s, positions[s], spot)
        mine = jnp.sum(jnp.where(lane == spot, back, 0.0), axis=1, keepdims=True)
        gtab[...] = jnp.broadcast_to(mine.astype(BF16).astype(F32), (SLOTS, ROW))
        g1[...] = jnp.zeros_like(g1)
        g2[...] = jnp.zeros_like(g2)
        g3[...] = jnp.zeros_like(g3)

    lane = iota((c1, n * ROW), 1) % ROW
    keep_after = (lane < ROW - 1).astype(F32).astype(BF16)
    keep_before = (lane > 0).astype(F32).astype(BF16)
    for c in range(px // (n * ROW)):
        at = pl.ds(c * n * ROW, n * ROW)
        scale = []
        for j in range(n):
            slot = slots[step * (px // ROW) + c * n + j]
            scale.append(jnp.broadcast_to(gtab[pl.ds(slot, 1), :], (16, ROW)).astype(BF16))
        scale = jnp.concatenate(scale, axis=1)
        tall = lambda count: jnp.concatenate([scale] * (count // 16), axis=0)
        c2 = d3_ref.shape[0]
        ds = ds_ref[:, at] * tall(c1)
        stack = jnp.concatenate(
            [roll_rows(ds, -1) * keep_after, ds, roll_rows(ds, 1) * keep_before], axis=0
        )
        g1[...] += mm_nt(stack, x_ref[:, at])
        g2[...] += mm_nt(dh2_ref[:, at] * tall(c2), a1_ref[:, at])
        g3[...] += mm_nt(d3_ref[:, at] * tall(c2), a2_ref[:, at])

    @pl.when(step == pl.num_programs(0) - 1)
    def _():
        head = jnp.sum(gtab[...] * heads[...], axis=0, keepdims=True)
        write_flat(
            g1[0:c1], g1[c1 : 2 * c1], g1[2 * c1 :], g2[...], g3[...], head, w1, taps, lo, hi, rows
        )


def backward(cty_dev, scalars, pixels, saved, heads, returned, w1, taps):
    ft, c1, c2 = pixels.shape[0], saved[0].shape[0], saved[1].shape[0]
    px = STEP_PX
    total = pixels.shape[1]
    cols = lambda ch: pl.BlockSpec((ch, px), lambda i, *s: (0, i))
    consts = (heads, *returned, w1, taps)
    return pl.pallas_call(
        functools.partial(backward_kernel, cty_dev),
        out_shape=jax.ShapeDtypeStruct((PIECES * PIECE // ROW, ROW), F32),
        grid_spec=pltpu.PrefetchScalarGridSpec(
            num_scalar_prefetch=4,
            grid=(total // px,),
            in_specs=[cols(v.shape[0]) for v in (pixels, *saved)]
            + [whole(w.shape) for w in consts],
            out_specs=whole((PIECES * PIECE // ROW, ROW)),
            scratch_shapes=[
                pltpu.VMEM((3 * c1, ft), F32),
                pltpu.VMEM((c2, c1), F32),
                pltpu.VMEM((c2, c2), F32),
                pltpu.VMEM((SLOTS, ROW), F32),
                pltpu.VMEM((c2, ROW), F32),
                pltpu.VMEM((c1, ROW), F32),
            ],
        ),
        compiler_params=pltpu.CompilerParams(dimension_semantics=("arbitrary",)),
        cost_estimate=pl.CostEstimate(
            flops=2 * total * 48000, bytes_accessed=25_000_000, transcendentals=0
        ),
        name="backward",
    )(*scalars, pixels, *saved, *consts)


def from_behind(value, by):
    peers = PIECES
    return lax.ppermute(value, TILE, [(i, (i + by) % peers) for i in range(peers)])


def swap(value, axes):
    return lax.all_to_all(value, axes, 0, 0, tiled=True)


def summed_everywhere(pieces):
    mine = jnp.sum(swap(pieces, TILE), axis=0)
    states = lax.axis_size("z")
    mine = jnp.sum(swap(jnp.broadcast_to(mine[None], (states, 1, PIECE)), ("z",)), axis=0)
    return swap(jnp.broadcast_to(mine[None], (PIECES, 1, PIECE)), TILE)


def on_device(
    bands, block_slot, tile_counties, county_place, label, w_first, taps, w_second, w_third, w_head
):
    pixels = bands[0]
    cty_dev = label.shape[1]
    devices = float(lax.axis_size("z") * PIECES)
    me = (lax.axis_index("x") * 4 + lax.axis_index("y")) * 2 + lax.axis_index("core")
    scalars = (block_slot[0], tile_counties[0], county_place[0], me.astype(jnp.int32)[None])
    *saved, heads, s0, s1, s2, s3 = forward(
        cty_dev, scalars, block_slot, pixels, w_first, taps, w_second.T, w_third, w_head[None, :]
    )
    sent = (s0, s1, s2, s3)
    got = [s0] + [from_behind(sent[k], k) for k in range(1, REACH)]
    county_mean, *back = settle(devices, got, label)
    returned = [back[0]] + [from_behind(back[k], -k) for k in range(1, REACH)]
    rows = backward(cty_dev, scalars, pixels, saved, heads, returned, w_first, taps)
    total = summed_everywhere(rows.reshape(PIECES, 1, PIECE))
    count = w_first.size + taps.size + w_second.size + w_third.size + w_head.size
    return county_mean, total.reshape(-1)[:count]


def solution(mesh):
    shape = mesh.devices.shape
    fine = Mesh(mesh.devices.reshape(shape[0], 4, 4, 2), ("z",) + TILE)
    in_specs = (
        P("z", None, TILE),
        P("z", TILE),
        P("z", TILE),
        P("z", None),
        P("z", TILE),
        P(),
        P(),
        P(),
        P(),
        P(),
    )
    return jax.shard_map(
        on_device, mesh=fine, in_specs=in_specs, out_specs=(P("z", TILE), P()), check_vma=False
    )
```

```python
import functools

import jax
import jax.numpy as jnp
from jax import lax
from jax.experimental import pallas as pl
from jax.experimental.pallas import tpu as pltpu
from jax.sharding import Mesh
from jax.sharding import PartitionSpec as P

MOST = 4
REACH = 4
ROW = 128
SLOTS = 8
PIECES = 32
PIECE = 1280
F32 = jnp.float32
BF16 = jnp.bfloat16
TILE = ("x", "y", "core")
FPX = 4096
BPX = 4096
WIDTH = 2
BW = 8
FLIM = 32000
BLIM = 20000


def mm(left, right):
    return jnp.dot(left, right, preferred_element_type=F32)


def mm_nt(left, right):
    return lax.dot_general(left, right, (((1,), (1,)), ((), ())), preferred_element_type=F32)


def iota(shape, axis):
    return lax.broadcasted_iota(jnp.int32, shape, axis)


def as_column(row, count):
    square = iota((count, count), 0) == iota((count, count), 1)
    return jnp.sum(jnp.where(square, row, 0.0), axis=1, keepdims=True)


def roll_rows(field, by):
    count = field.shape[1] // ROW
    parts = [pltpu.roll(field[:, i * ROW : (i + 1) * ROW], by % ROW, 1) for i in range(count)]
    return parts[0] if count == 1 else jnp.concatenate(parts, axis=1)


def wide(field, count):
    return field if count == 1 else jnp.concatenate([field] * count, axis=1)


def gate(half):
    plus = 1.0 + jnp.tanh(half)
    out = half * plus
    low, plus = out.astype(BF16), plus.astype(BF16)
    return out, low, plus + low * (2.0 - plus)


def in_hbm(*arrays):
    return tuple(pltpu.with_memory_space_constraint(a, pltpu.HBM) for a in arrays)


def whole(shape):
    zeros = (0,) * len(shape)
    return pl.BlockSpec(shape, lambda i, *s: zeros)


def slot_positions(counties, table, me, cty_dev):
    owners, codes, positions = [], [], []
    for s in range(SLOTS):
        place = table[0, counties[0, s]]
        owner = lax.div(place, cty_dev)
        rank = jnp.int32(0)
        for other in owners:
            rank = rank + (other == owner).astype(jnp.int32)
        owners.append(owner)
        codes.append(place - owner * cty_dev + 1)
        positions.append(lax.rem(owner - me[0, 0] + PIECES, PIECES) * MOST + rank)
    return positions, codes


def forward_kernel(
    cty_dev, slots, counties, table, me,
    x_ref, slotv, w1, taps, w2t, w3, wh,
    a1_ref, a2_ref, d3_ref, dh2_ref, ds_ref, heads_ref, s0, s1_, s2_, s3_,
    tapm, w2h, w3h, w2th, w3th, whb, whf, acc, q1, q2,
):
    step = pl.program_id(0)
    c2, c1 = w3.shape[0], w2t.shape[0]

    @pl.when(step == 0)
    def _():
        lane = iota((c1, ROW), 1)
        for k in range(3):
            col = jnp.broadcast_to(0.5 * as_column(taps[k : k + 1, :], c1), (c1, ROW))
            if k == 0:
                col = jnp.where(lane > 0, col, 0.0)
            if k == 2:
                col = jnp.where(lane < ROW - 1, col, 0.0)
            tapm[k] = col
        half2t = 0.5 * w2t[...].astype(F32)
        half3 = 0.5 * w3[...].astype(F32)
        w2th[...] = half2t.astype(BF16)
        w2h[...] = jnp.transpose(half2t).astype(BF16)
        w3h[...] = half3.astype(BF16)
        w3th[...] = jnp.transpose(half3).astype(BF16)
        col = jnp.broadcast_to(0.5 * as_column(wh[...].astype(F32), c2), (c2, ROW))
        whf[...] = col
        whb[...] = col.astype(BF16)
        acc[...] = jnp.zeros_like(acc)

    px = x_ref.shape[1]
    spans = [pl.ds(c * WIDTH * ROW, WIDTH * ROW) for c in range(px // (WIDTH * ROW))]
    n = WIDTH
    for at in spans:
        h1 = mm(w1[...], x_ref[:, at])
        s1 = wide(tapm[0], n) * roll_rows(h1, 1) + wide(tapm[1], n) * h1
        s1 = s1 + wide(tapm[2], n) * roll_rows(h1, -1)
        _, a1_ref[:, at], q1[:, at] = gate(s1)
    for at in spans:
        _, a2_ref[:, at], q2[:, at] = gate(mm(w2h[...], a1_ref[:, at]))
    heads = jnp.zeros(acc.shape, F32)
    for c, at in enumerate(spans):
        a2 = a2_ref[:, at]
        out, _, q3 = gate(mm(w3h[...], a2))
        d3_ref[:, at] = wide(whb[...], n) * q3
        a3 = (out + a2.astype(F32)).astype(BF16)
        member = []
        for j in range(n):
            slot = slots[0, step * (px // ROW) + c * n + j]
            member.append((iota(acc.shape, 0) == slot).astype(F32).astype(BF16))
        heads = heads + mm_nt(jnp.concatenate(member, axis=1), a3)
    for at in spans:
        back = mm(w3th[...], d3_ref[:, at]) + wide(whf[...], n)
        dh2_ref[:, at] = back.astype(BF16) * q2[:, at]
    for at in spans:
        ds_ref[:, at] = mm(w2th[...], dh2_ref[:, at]).astype(BF16) * q1[:, at]
    acc[...] += heads

    @pl.when(step == pl.num_programs(0) - 1)
    def _():
        per_slot = acc[0:SLOTS, :]
        heads_ref[...] = per_slot
        sums = jnp.sum(per_slot * wh[...].astype(F32), axis=1, keepdims=True)
        counts = (slotv[...] == iota((SLOTS, slotv.shape[1]), 0)).astype(F32)
        counts = jnp.sum(counts, axis=1, keepdims=True) * float(ROW)
        positions, codes = slot_positions(counties, table, me, cty_dev)
        lane = iota((SLOTS, ROW), 1)
        row = iota((SLOTS, ROW), 0)
        packed = jnp.zeros((SLOTS, ROW), F32)
        for s in range(SLOTS):
            value = jnp.where(row == 0, sums[s : s + 1, :], counts[s : s + 1, :])
            value = jnp.where(row == 2, codes[s].astype(F32), value)
            packed = jnp.where(lane == positions[s], value, packed)
        for k, ref in enumerate((s0, s1_, s2_, s3_)):
            ref[...] = pltpu.roll(packed, (-MOST * k) % ROW, 1)


def forward(cty_dev, scalars, slotv, pixels, w1, taps, w2t, w3, wh):
    total = pixels.shape[1]
    c1, c2 = w2t.shape[0], w2t.shape[1]
    chans = [c1, c2, c2, c2, c1]
    px = FPX
    scalar_specs = [pl.BlockSpec(memory_space=pltpu.SMEM)] * len(scalars)
    cols = lambda ch: pl.BlockSpec((ch, px), lambda i, *s: (0, i))
    (pixels,) = in_hbm(pixels)
    consts = in_hbm(slotv, w1, taps, w2t, w3, wh)
    small = [(SLOTS, c2)] + [(SLOTS, ROW)] * REACH
    return pl.pallas_call(
        functools.partial(forward_kernel, cty_dev),
        out_shape=[jax.ShapeDtypeStruct((ch, total), BF16) for ch in chans]
        + [jax.ShapeDtypeStruct(s, F32) for s in small],
        grid_spec=pltpu.PrefetchScalarGridSpec(
            num_scalar_prefetch=0,
            grid=(total // px,),
            in_specs=scalar_specs + [cols(pixels.shape[0])] + [whole(w.shape) for w in consts],
            out_specs=[cols(ch) for ch in chans] + [whole(s) for s in small],
            scratch_shapes=[
                pltpu.VMEM((3, c1, ROW), F32),
                pltpu.VMEM((c2, c1), BF16),
                pltpu.VMEM((c2, c2), BF16),
                pltpu.VMEM((c1, c2), BF16),
                pltpu.VMEM((c2, c2), BF16),
                pltpu.VMEM((c2, ROW), BF16),
                pltpu.VMEM((c2, ROW), F32),
                pltpu.VMEM((16, c2), F32),
                pltpu.VMEM((c1, px), BF16),
                pltpu.VMEM((c2, px), BF16),
            ],
        ),
        compiler_params=pltpu.CompilerParams(
            dimension_semantics=("arbitrary",), vmem_limit_bytes=FLIM * 1024
        ),
        cost_estimate=pl.CostEstimate(
            flops=2 * total * 75000, bytes_accessed=25_000_000, transcendentals=total * 320
        ),
        name="forward",
    )(*scalars, pixels, *consts)


def settle_kernel(devices, cty_dev, p0, p1, p2, p3, label, mean_ref, b0, b1, b2, b3):
    size = 16
    lane = iota((SLOTS, ROW), 1)
    got = jnp.zeros((SLOTS, ROW), F32)
    for k, ref in enumerate((p0, p1, p2, p3)):
        moved = pltpu.roll(ref[...], MOST * k, 1) if k else ref[...]
        got = jnp.where((lane >= MOST * k) & (lane < MOST * (k + 1)), moved, got)
    owned = iota((size, ROW), 0)
    hit = (got[2:3, :] == (owned + 1).astype(F32)) & (owned < cty_dev)
    total = jnp.sum(jnp.where(hit, got[0:1, :], 0.0), axis=1, keepdims=True)
    number = jnp.sum(jnp.where(hit, got[1:2, :], 0.0), axis=1, keepdims=True)
    same = owned == iota((size, ROW), 1)
    labels = jnp.concatenate(
        [label[...].astype(F32), jnp.zeros((1, ROW - label.shape[1]), F32)], axis=1
    )
    target = jnp.sum(jnp.where(same, labels, 0.0), axis=1, keepdims=True) * 0.01
    denom = jnp.maximum(number, 1.0)
    mean = total / denom
    live = jnp.where(number > 0.5, 2.0, 0.0)
    adjoint = live * (mean - target) / (devices * denom)
    spread = jnp.sum(jnp.where(same, mean, 0.0), axis=0, keepdims=True)
    mean_ref[...] = spread[:, :cty_dev]
    back = jnp.sum(jnp.where(hit, adjoint, 0.0), axis=0, keepdims=True)
    back = jnp.broadcast_to(back, (SLOTS, ROW))
    for k, ref in enumerate((b0, b1, b2, b3)):
        ref[...] = pltpu.roll(back, (-MOST * k) % ROW, 1)


def settle(devices, pieces, label):
    cty_dev = label.shape[1]
    tile = jax.ShapeDtypeStruct((SLOTS, ROW), F32)
    return pl.pallas_call(
        functools.partial(settle_kernel, devices, cty_dev),
        out_shape=[jax.ShapeDtypeStruct((1, cty_dev), F32)] + [tile] * REACH,
        compiler_params=pltpu.CompilerParams(vmem_limit_bytes=1024 * 1024),
        name="settle",
    )(*pieces, label)


def write_flat(after, same, before, second, third, head, w1, taps, lo, hi, rows):
    c1, ft = w1.shape
    cols = [as_column(taps[k : k + 1, :], c1) for k in range(3)]
    first = cols[0] * after + cols[1] * same + cols[2] * before
    lo[0:c1, :] = first[:, :ROW]
    hi[...] = jnp.zeros_like(hi)
    hi[:, 0 : ft - ROW] = first[:, ROW:]
    filled = 15
    lane = iota((8, ROW), 1)
    for p in range(filled):
        src, at = divmod(p * ROW, ft)
        near = pl.ds(src, 8, stride=8)
        piece = jnp.concatenate([lo[near, :], hi[near, :]], axis=1)
        piece = pltpu.roll(piece, (-at) % 256, 1)[:, :ROW] if at else piece[:, :ROW]
        left = ft - at
        if left < ROW:
            far = lo[pl.ds(src + 1, 8, stride=8), :]
            piece = jnp.where(lane < left, piece, pltpu.roll(far, left, 1))
        rows[pl.ds(p, 8, stride=filled), :] = piece
    base = c1 * ft // ROW
    half = ROW // 2
    wf = w1[...].astype(F32)
    t0, t1, t2 = [
        jnp.sum(jnp.transpose(wf * part), axis=0, keepdims=True) for part in (after, same, before)
    ]
    c2 = second.shape[0]
    rows[base : base + 1, :] = jnp.concatenate([t0, t1], axis=1)
    lo[:, 0:half] = second
    even = lo[pl.ds(0, c2 // 2, stride=2), :]
    odd = lo[pl.ds(1, c2 // 2, stride=2), :]
    low = iota((c2, ROW), 1) < half
    rows[base + 2 : base + 1 + c2 // 2, :] = jnp.where(
        low[: c2 // 2 - 1], odd[: c2 // 2 - 1], pltpu.roll(even, half, 1)[1:]
    )
    rows[base + 1 : base + 2, :] = jnp.concatenate([t2, second[0:1]], axis=1)
    mark = base + 1 + c2 // 2
    turned = pltpu.roll(third, half, 1)
    rows[mark : mark + 1, :] = jnp.where(low[0:1], odd[c2 // 2 - 1 :], turned[0:1])
    rows[mark + 1 : mark + c2, :] = jnp.where(low[1:], turned[: c2 - 1], turned[1:])
    turned_head = pltpu.roll(head, half, 1)
    rows[mark + c2 : mark + c2 + 1, :] = jnp.where(low[0:1], turned[c2 - 1 :], turned_head)
    rows[mark + c2 + 1 : mark + c2 + 2, :] = jnp.where(low[0:1], turned_head, 0.0)
    rest = rows.shape[0] - (mark + c2 + 2)
    rows[mark + c2 + 2 :, :] = jnp.zeros((rest, ROW), F32)


def backward_kernel(
    cty_dev, slots, counties, table, me,
    x_ref, a1_ref, a2_ref, d3_ref, dh2_ref, ds_ref, heads, r0, r1, r2, r3, w1, taps,
    rows, g1, g2, g3, gtab, lo, hi,
):
    step = pl.program_id(0)
    c1 = a1_ref.shape[0]
    px = x_ref.shape[1]
    n = BW

    @pl.when(step == 0)
    def _():
        lane = iota((SLOTS, ROW), 1)
        back = jnp.zeros((SLOTS, ROW), F32)
        for k, ref in enumerate((r0, r1, r2, r3)):
            moved = pltpu.roll(ref[...], MOST * k, 1) if k else ref[...]
            back = jnp.where((lane >= MOST * k) & (lane < MOST * (k + 1)), moved, back)
        positions, _ = slot_positions(counties, table, me, cty_dev)
        row = iota((SLOTS, ROW), 0)
        spot = jnp.zeros((SLOTS, ROW), jnp.int32)
        for s in range(SLOTS):
            spot = jnp.where(row == s, positions[s], spot)
        mine = jnp.sum(jnp.where(lane == spot, back, 0.0), axis=1, keepdims=True)
        gtab[...] = jnp.broadcast_to(mine.astype(BF16).astype(F32), (SLOTS, ROW))
        g1[...] = jnp.zeros_like(g1)
        g2[...] = jnp.zeros_like(g2)
        g3[...] = jnp.zeros_like(g3)

    lane = iota((c1, n * ROW), 1) % ROW
    keep_after = (lane < ROW - 1).astype(F32).astype(BF16)
    keep_before = (lane > 0).astype(F32).astype(BF16)
    for c in range(px // (n * ROW)):
        at = pl.ds(c * n * ROW, n * ROW)
        scale = []
        for j in range(n):
            slot = slots[0, step * (px // ROW) + c * n + j]
            scale.append(jnp.broadcast_to(gtab[pl.ds(slot, 1), :], (16, ROW)).astype(BF16))
        scale = jnp.concatenate(scale, axis=1)
        tall = lambda count: jnp.concatenate([scale] * (count // 16), axis=0)
        c2 = d3_ref.shape[0]
        ds = ds_ref[:, at] * tall(c1)
        stack = jnp.concatenate(
            [roll_rows(ds, -1) * keep_after, ds, roll_rows(ds, 1) * keep_before], axis=0
        )
        g1[...] += mm_nt(stack, x_ref[:, at])
        g2[...] += mm_nt(dh2_ref[:, at] * tall(c2), a1_ref[:, at])
        g3[...] += mm_nt(d3_ref[:, at] * tall(c2), a2_ref[:, at])

    @pl.when(step == pl.num_programs(0) - 1)
    def _():
        head = jnp.sum(gtab[...] * heads[...], axis=0, keepdims=True)
        write_flat(
            g1[0:c1], g1[c1 : 2 * c1], g1[2 * c1 :], g2[...], g3[...], head, w1, taps, lo, hi, rows
        )


def backward(cty_dev, scalars, pixels, saved, heads, returned, w1, taps):
    ft, c1, c2 = pixels.shape[0], saved[0].shape[0], saved[1].shape[0]
    px = BPX
    scalar_specs = [pl.BlockSpec(memory_space=pltpu.SMEM)] * len(scalars)
    total = pixels.shape[1]
    cols = lambda ch: pl.BlockSpec((ch, px), lambda i, *s: (0, i))
    (pixels,) = in_hbm(pixels)
    consts = (heads, *returned, *in_hbm(w1, taps))
    return pl.pallas_call(
        functools.partial(backward_kernel, cty_dev),
        out_shape=jax.ShapeDtypeStruct((PIECES * PIECE // ROW, ROW), F32),
        grid_spec=pltpu.PrefetchScalarGridSpec(
            num_scalar_prefetch=0,
            grid=(total // px,),
            in_specs=scalar_specs + [cols(v.shape[0]) for v in (pixels, *saved)]
            + [whole(w.shape) for w in consts],
            out_specs=whole((PIECES * PIECE // ROW, ROW)),
            scratch_shapes=[
                pltpu.VMEM((3 * c1, ft), F32),
                pltpu.VMEM((c2, c1), F32),
                pltpu.VMEM((c2, c2), F32),
                pltpu.VMEM((SLOTS, ROW), F32),
                pltpu.VMEM((c2, ROW), F32),
                pltpu.VMEM((c1, ROW), F32),
            ],
        ),
        compiler_params=pltpu.CompilerParams(
            dimension_semantics=("arbitrary",), vmem_limit_bytes=BLIM * 1024
        ),
        cost_estimate=pl.CostEstimate(
            flops=2 * total * 48000, bytes_accessed=25_000_000, transcendentals=0
        ),
        name="backward",
    )(*scalars, pixels, *saved, *consts)


def from_behind(value, by):
    peers = PIECES
    return lax.ppermute(value, TILE, [(i, (i + by) % peers) for i in range(peers)])


def swap(value, axes):
    return lax.all_to_all(value, axes, 0, 0, tiled=True)


def summed_everywhere(pieces):
    mine = jnp.sum(swap(pieces, TILE), axis=0)
    states = lax.axis_size("z")
    mine = jnp.sum(swap(jnp.broadcast_to(mine[None], (states, 1, PIECE)), ("z",)), axis=0)
    return swap(jnp.broadcast_to(mine[None], (PIECES, 1, PIECE)), TILE)


def on_device(
    bands, block_slot, tile_counties, county_place, label, w_first, taps, w_second, w_third, w_head
):
    pixels = bands[0]
    cty_dev = label.shape[1]
    devices = float(lax.axis_size("z") * PIECES)
    me = (lax.axis_index("x") * 4 + lax.axis_index("y")) * 2 + lax.axis_index("core")
    scalars = (*in_hbm(block_slot, tile_counties, county_place), me.astype(jnp.int32)[None, None])
    *saved, heads, s0, s1, s2, s3 = forward(
        cty_dev, scalars, block_slot, pixels, w_first, taps, w_second.T, w_third, w_head[None, :]
    )
    sent = (s0, s1, s2, s3)
    got = [s0] + [from_behind(sent[k], k) for k in range(1, REACH)]
    county_mean, *back = settle(devices, got, label)
    returned = [back[0]] + [from_behind(back[k], -k) for k in range(1, REACH)]
    rows = backward(cty_dev, scalars, pixels, saved, heads, returned, w_first, taps)
    total = summed_everywhere(rows.reshape(PIECES, 1, PIECE))
    count = w_first.size + taps.size + w_second.size + w_third.size + w_head.size
    return county_mean, total.reshape(-1)[:count]


def solution(mesh):
    shape = mesh.devices.shape
    fine = Mesh(mesh.devices.reshape(shape[0], 4, 4, 2), ("z",) + TILE)
    in_specs = (
        P("z", None, TILE),
        P("z", TILE),
        P("z", TILE),
        P("z", None),
        P("z", TILE),
        P(),
        P(),
        P(),
        P(),
        P(),
    )
    return jax.shard_map(
        on_device, mesh=fine, in_specs=in_specs, out_specs=(P("z", TILE), P()), check_vma=False
    )
```

```python
import functools

import jax
import jax.numpy as jnp
from jax import lax
from jax.experimental import pallas as pl
from jax.experimental.pallas import tpu as pltpu
from jax.sharding import Mesh
from jax.sharding import PartitionSpec as P

REACH = 4
ROW = 128
SLOTS = 8
PIECES = 32
PIECE = 1280
F32 = jnp.float32
BF16 = jnp.bfloat16
TILE = ("x", "y", "core")
FPX = 4096
BPX = 4096
WIDTH = 2
BW = 8
CPX = 4096
FLIM = 24000
BLIM = 20000
CLIM = 20000


def mm(left, right):
    return jnp.dot(left, right, preferred_element_type=F32)


def mm_nt(left, right):
    return lax.dot_general(left, right, (((1,), (1,)), ((), ())), preferred_element_type=F32)


def iota(shape, axis):
    return lax.broadcasted_iota(jnp.int32, shape, axis)


def as_column(row, count):
    square = iota((count, count), 0) == iota((count, count), 1)
    return jnp.sum(jnp.where(square, row, 0.0), axis=1, keepdims=True)


def roll_rows(field, by):
    count = field.shape[1] // ROW
    parts = [pltpu.roll(field[:, i * ROW : (i + 1) * ROW], by % ROW, 1) for i in range(count)]
    return parts[0] if count == 1 else jnp.concatenate(parts, axis=1)


def wide(field, count):
    return field if count == 1 else jnp.concatenate([field] * count, axis=1)


def gate(half):
    plus = 1.0 + jnp.tanh(half)
    out = half * plus
    return out, out.astype(BF16), plus.astype(BF16)


def slope(low, plus):
    return plus + low * (2.0 - plus)


def in_hbm(*arrays):
    return tuple(pltpu.with_memory_space_constraint(a, pltpu.HBM) for a in arrays)


def whole(shape):
    zeros = (0,) * len(shape)
    return pl.BlockSpec(shape, lambda i, *s: zeros)


def forward_kernel(
    cty_dev, slots, counties, table, me, x_ref, slotv, label, w1, taps, w2t, w3, wh,
    a1_ref, a2_ref, l3_ref, p1, p2, p3, heads_ref, packet,
    tapm, w2h, w3h, acc,
):
    step = pl.program_id(0)
    c2, c1 = w3.shape[0], w2t.shape[0]

    @pl.when(step == 0)
    def _():
        lane = iota((c1, ROW), 1)
        for k in range(3):
            col = jnp.broadcast_to(0.5 * as_column(taps[k : k + 1, :], c1), (c1, ROW))
            if k == 0:
                col = jnp.where(lane > 0, col, 0.0)
            if k == 2:
                col = jnp.where(lane < ROW - 1, col, 0.0)
            tapm[k] = col
        w2h[...] = jnp.transpose(0.5 * w2t[...].astype(F32)).astype(BF16)
        w3h[...] = (0.5 * w3[...].astype(F32)).astype(BF16)
        acc[...] = jnp.zeros_like(acc)

    px = x_ref.shape[1]
    spans = [pl.ds(c * WIDTH * ROW, WIDTH * ROW) for c in range(px // (WIDTH * ROW))]
    n = WIDTH
    for at in spans:
        h1 = mm(w1[...], x_ref[:, at])
        s1 = wide(tapm[0], n) * roll_rows(h1, 1) + wide(tapm[1], n) * h1
        s1 = s1 + wide(tapm[2], n) * roll_rows(h1, -1)
        _, a1_ref[:, at], p1[:, at] = gate(s1)
    for at in spans:
        _, a2_ref[:, at], p2[:, at] = gate(mm(w2h[...], a1_ref[:, at]))
    heads = jnp.zeros(acc.shape, F32)
    for c, at in enumerate(spans):
        a2 = a2_ref[:, at]
        out, l3_ref[:, at], p3[:, at] = gate(mm(w3h[...], a2))
        a3 = (out + a2.astype(F32)).astype(BF16)
        member = []
        for j in range(n):
            slot = slots[0, step * (px // ROW) + c * n + j]
            member.append((iota(acc.shape, 0) == slot).astype(F32).astype(BF16))
        heads = heads + mm_nt(jnp.concatenate(member, axis=1), a3)
    acc[...] += heads

    @pl.when(step == pl.num_programs(0) - 1)
    def _():
        per_slot = acc[0:SLOTS, :]
        heads_ref[...] = per_slot
        sums = jnp.sum(per_slot * wh[...].astype(F32), axis=1, keepdims=True)
        counts = (slotv[...] == iota((SLOTS, slotv.shape[1]), 0)).astype(F32)
        counts = jnp.sum(counts, axis=1, keepdims=True) * float(ROW)
        blank = jnp.zeros((1, ROW), F32)
        codes, spots, lane = blank, blank, iota((1, ROW), 1)
        for s in range(SLOTS):
            place = table[0, counties[0, s]]
            owner = lax.div(place, cty_dev)
            spot = cty_dev * lax.rem(owner - me[0, 0] + PIECES, PIECES) + place - cty_dev * owner
            codes = jnp.where(lane == s, (place + 1).astype(F32), codes)
            spots = jnp.where(lane == s, spot.astype(F32), spots)
        base = jnp.zeros((1, ROW), jnp.int32) + (cty_dev * me[0, 0] + 1)
        own = label[...].astype(F32)
        own = jnp.concatenate([own, jnp.zeros((1, ROW - own.shape[1]), F32)], axis=1)
        slot_lane = iota((SLOTS, ROW), 0) == iota((SLOTS, ROW), 1)
        as_row = lambda col: jnp.sum(jnp.where(slot_lane, col, 0.0), axis=0, keepdims=True)
        packet[...] = jnp.concatenate(
            [as_row(sums), as_row(counts), codes, own, spots, base.astype(F32), blank, blank]
        )


def forward(cty_dev, scalars, slotv, label, pixels, w1, taps, w2t, w3, wh):
    total = pixels.shape[1]
    c1, c2 = w2t.shape[0], w2t.shape[1]
    chans = [c1, c2, c2, c1, c2, c2]
    px = FPX
    scalar_specs = [pl.BlockSpec(memory_space=pltpu.SMEM)] * len(scalars)
    cols = lambda ch: pl.BlockSpec((ch, px), lambda i, *s: (0, i))
    (pixels,) = in_hbm(pixels)
    consts = in_hbm(slotv, label, w1, taps, w2t, w3, wh)
    small = [(SLOTS, c2), (SLOTS, ROW)]
    return pl.pallas_call(
        functools.partial(forward_kernel, cty_dev),
        out_shape=[jax.ShapeDtypeStruct((ch, total), BF16) for ch in chans]
        + [jax.ShapeDtypeStruct(s, F32) for s in small],
        grid_spec=pltpu.PrefetchScalarGridSpec(
            num_scalar_prefetch=0,
            grid=(total // px,),
            in_specs=scalar_specs + [cols(pixels.shape[0])] + [whole(w.shape) for w in consts],
            out_specs=[cols(ch) for ch in chans] + [whole(s) for s in small],
            scratch_shapes=[
                pltpu.VMEM((3, c1, ROW), F32),
                pltpu.VMEM((c2, c1), BF16),
                pltpu.VMEM((c2, c2), BF16),
                pltpu.VMEM((16, c2), F32),
            ],
        ),
        compiler_params=pltpu.CompilerParams(
            dimension_semantics=("arbitrary",), vmem_limit_bytes=FLIM * 1024
        ),
        cost_estimate=pl.CostEstimate(
            flops=2 * total * 42000, bytes_accessed=25_000_000, transcendentals=total * 320
        ),
        name="forward",
    )(*scalars, pixels, *consts)


def chain_kernel(
    a1_ref, a2_ref, l3_ref, p1, p2, p3, w2t, w3, wh, d3_ref, dh2_ref, ds_ref, w2th, w3th, whf, whb
):
    c2 = w3.shape[0]
    n = WIDTH

    @pl.when(pl.program_id(0) == 0)
    def _():
        w2th[...] = (0.5 * w2t[...].astype(F32)).astype(BF16)
        w3th[...] = jnp.transpose(0.5 * w3[...].astype(F32)).astype(BF16)
        col = jnp.broadcast_to(0.5 * as_column(wh[...].astype(F32), c2), (c2, ROW))
        whf[...] = col
        whb[...] = col.astype(BF16)

    px = a1_ref.shape[1]
    spans = [pl.ds(c * n * ROW, n * ROW) for c in range(px // (n * ROW))]
    for at in spans:
        d3_ref[:, at] = wide(whb[...], n) * slope(l3_ref[:, at], p3[:, at])
    for at in spans:
        back = mm(w3th[...], d3_ref[:, at]) + wide(whf[...], n)
        dh2_ref[:, at] = back.astype(BF16) * slope(a2_ref[:, at], p2[:, at])
    for at in spans:
        back = mm(w2th[...], dh2_ref[:, at])
        ds_ref[:, at] = back.astype(BF16) * slope(a1_ref[:, at], p1[:, at])


def chain(saved, w2t, w3, wh):
    c1, total = saved[0].shape
    c2 = w3.shape[0]
    px = CPX
    cols = lambda ch: pl.BlockSpec((ch, px), lambda i, *s: (0, i))
    consts = in_hbm(w2t, w3, wh)
    return pl.pallas_call(
        chain_kernel,
        out_shape=[jax.ShapeDtypeStruct((ch, total), BF16) for ch in (c2, c2, c1)],
        grid=(total // px,),
        in_specs=[cols(v.shape[0]) for v in saved] + [whole(w.shape) for w in consts],
        out_specs=[cols(c2), cols(c2), cols(c1)],
        scratch_shapes=[
            pltpu.VMEM((c1, c2), BF16),
            pltpu.VMEM((c2, c2), BF16),
            pltpu.VMEM((c2, ROW), F32),
            pltpu.VMEM((c2, ROW), BF16),
        ],
        compiler_params=pltpu.CompilerParams(
            dimension_semantics=("arbitrary",), vmem_limit_bytes=CLIM * 1024
        ),
        cost_estimate=pl.CostEstimate(
            flops=2 * total * 25000, bytes_accessed=17_000_000, transcendentals=0
        ),
        name="chain",
    )(*saved, *consts)


def settle(devices, cty_dev, packets, mean_ref):
    lane = iota((SLOTS, ROW), 1)
    got = jnp.zeros((SLOTS, ROW), F32)
    labels = jnp.zeros((1, ROW), F32)
    far = REACH - 1
    for k, ref in enumerate(packets):
        packet = ref[...]
        moved = pltpu.roll(packet, SLOTS * k, 1) if k else packet
        got = jnp.where((lane >= SLOTS * k) & (lane < SLOTS * (k + 1)), moved, got)
        if k >= far:
            at = cty_dev * (k - far)
            row = packet[3:4, :]
            row = pltpu.roll(row, at, 1) if at else row
            here = lane[0:1, :]
            labels = jnp.where((here >= at) & (here < at + cty_dev), row, labels)
    sums, counts, codes = got[0:1, :], got[1:2, :], got[2:3, :]
    own = packets[far][...]
    code = as_column(own[2:3, :SLOTS], SLOTS)
    spot = as_column(own[4:5, :SLOTS], SLOTS)

    def mean_of(hit):
        total = jnp.sum(jnp.where(hit, sums, 0.0), axis=1, keepdims=True)
        number = jnp.sum(jnp.where(hit, counts, 0.0), axis=1, keepdims=True)
        denom = jnp.maximum(number, 1.0)
        return total / denom, number, denom

    mean, number, denom = mean_of(codes == code)
    target = jnp.sum(jnp.where(lane.astype(F32) == spot, labels, 0.0), axis=1, keepdims=True) * 0.01
    live = jnp.where(number > 0.5, 2.0, 0.0)
    adjoint = live * (mean - target) / (devices * denom)
    owned = iota((16, ROW), 0)
    mine = (codes == owned.astype(F32) + own[5:6, :]) & (owned < cty_dev)
    mean, _, _ = mean_of(mine)
    spread = jnp.sum(jnp.where(owned == iota((16, ROW), 1), mean, 0.0), axis=0, keepdims=True)
    mean_ref[...] = spread[:, :cty_dev]
    return adjoint


def write_flat(after, same, before, second, third, head, w1, taps, lo, hi, rows):
    c1, ft = w1.shape
    cols = [as_column(taps[k : k + 1, :], c1) for k in range(3)]
    first = cols[0] * after + cols[1] * same + cols[2] * before
    lo[0:c1, :] = first[:, :ROW]
    hi[...] = jnp.zeros_like(hi)
    hi[:, 0 : ft - ROW] = first[:, ROW:]
    filled = 15
    lane = iota((8, ROW), 1)
    for p in range(filled):
        src, at = divmod(p * ROW, ft)
        near = pl.ds(src, 8, stride=8)
        piece = jnp.concatenate([lo[near, :], hi[near, :]], axis=1)
        piece = pltpu.roll(piece, (-at) % 256, 1)[:, :ROW] if at else piece[:, :ROW]
        left = ft - at
        if left < ROW:
            far = lo[pl.ds(src + 1, 8, stride=8), :]
            piece = jnp.where(lane < left, piece, pltpu.roll(far, left, 1))
        rows[pl.ds(p, 8, stride=filled), :] = piece
    base = c1 * ft // ROW
    half = ROW // 2
    wf = w1[...].astype(F32)
    t0, t1, t2 = [
        jnp.sum(jnp.transpose(wf * part), axis=0, keepdims=True) for part in (after, same, before)
    ]
    c2 = second.shape[0]
    rows[base : base + 1, :] = jnp.concatenate([t0, t1], axis=1)
    lo[:, 0:half] = second
    even = lo[pl.ds(0, c2 // 2, stride=2), :]
    odd = lo[pl.ds(1, c2 // 2, stride=2), :]
    low = iota((c2, ROW), 1) < half
    rows[base + 2 : base + 1 + c2 // 2, :] = jnp.where(
        low[: c2 // 2 - 1], odd[: c2 // 2 - 1], pltpu.roll(even, half, 1)[1:]
    )
    rows[base + 1 : base + 2, :] = jnp.concatenate([t2, second[0:1]], axis=1)
    mark = base + 1 + c2 // 2
    turned = pltpu.roll(third, half, 1)
    rows[mark : mark + 1, :] = jnp.where(low[0:1], odd[c2 // 2 - 1 :], turned[0:1])
    rows[mark + 1 : mark + c2, :] = jnp.where(low[1:], turned[: c2 - 1], turned[1:])
    turned_head = pltpu.roll(head, half, 1)
    rows[mark + c2 : mark + c2 + 1, :] = jnp.where(low[0:1], turned[c2 - 1 :], turned_head)
    rows[mark + c2 + 1 : mark + c2 + 2, :] = jnp.where(low[0:1], turned_head, 0.0)
    rest = rows.shape[0] - (mark + c2 + 2)
    rows[mark + c2 + 2 :, :] = jnp.zeros((rest, ROW), F32)


def backward_kernel(
    devices, cty_dev, slots, x_ref, a1_ref, a2_ref, d3_ref, dh2_ref, ds_ref, heads, k0, k1, k2, k3, k4, k5, k6, w1, taps,
    rows, mean_ref, g1, g2, g3, gtab, lo, hi,
):
    step = pl.program_id(0)
    c1 = a1_ref.shape[0]
    px = x_ref.shape[1]
    n = BW

    @pl.when(step == 0)
    def _():
        packets = (k0, k1, k2, k3, k4, k5, k6)
        mine = settle(devices, cty_dev, packets, mean_ref)
        gtab[...] = jnp.broadcast_to(mine.astype(BF16).astype(F32), (SLOTS, ROW))
        g1[...] = jnp.zeros_like(g1)
        g2[...] = jnp.zeros_like(g2)
        g3[...] = jnp.zeros_like(g3)

    lane = iota((c1, n * ROW), 1) % ROW
    keep_after = (lane < ROW - 1).astype(F32).astype(BF16)
    keep_before = (lane > 0).astype(F32).astype(BF16)
    for c in range(px // (n * ROW)):
        at = pl.ds(c * n * ROW, n * ROW)
        scale = []
        for j in range(n):
            slot = slots[0, step * (px // ROW) + c * n + j]
            scale.append(jnp.broadcast_to(gtab[pl.ds(slot, 1), :], (16, ROW)).astype(BF16))
        scale = jnp.concatenate(scale, axis=1)
        tall = lambda count: jnp.concatenate([scale] * (count // 16), axis=0)
        c2 = d3_ref.shape[0]
        ds = ds_ref[:, at] * tall(c1)
        stack = jnp.concatenate(
            [roll_rows(ds, -1) * keep_after, ds, roll_rows(ds, 1) * keep_before], axis=0
        )
        g1[...] += mm_nt(stack, x_ref[:, at])
        g2[...] += mm_nt(dh2_ref[:, at] * tall(c2), a1_ref[:, at])
        g3[...] += mm_nt(d3_ref[:, at] * tall(c2), a2_ref[:, at])

    @pl.when(step == pl.num_programs(0) - 1)
    def _():
        head = jnp.sum(gtab[...] * heads[...], axis=0, keepdims=True)
        write_flat(
            g1[0:c1], g1[c1 : 2 * c1], g1[2 * c1 :], g2[...], g3[...], head, w1, taps, lo, hi, rows
        )


def backward(devices, cty_dev, scalars, pixels, saved, heads, packets, w1, taps):
    ft, c1, c2 = pixels.shape[0], saved[0].shape[0], saved[1].shape[0]
    px = BPX
    scalar_specs = [pl.BlockSpec(memory_space=pltpu.SMEM)] * len(scalars)
    total = pixels.shape[1]
    cols = lambda ch: pl.BlockSpec((ch, px), lambda i, *s: (0, i))
    (pixels,) = in_hbm(pixels)
    consts = (heads, *packets, *in_hbm(w1, taps))
    return pl.pallas_call(
        functools.partial(backward_kernel, devices, cty_dev),
        out_shape=[
            jax.ShapeDtypeStruct((PIECES * PIECE // ROW, ROW), F32),
            jax.ShapeDtypeStruct((1, cty_dev), F32),
        ],
        grid_spec=pltpu.PrefetchScalarGridSpec(
            num_scalar_prefetch=0,
            grid=(total // px,),
            in_specs=scalar_specs + [cols(v.shape[0]) for v in (pixels, *saved)]
            + [whole(w.shape) for w in consts],
            out_specs=[whole((PIECES * PIECE // ROW, ROW)), whole((1, cty_dev))],
            scratch_shapes=[
                pltpu.VMEM((3 * c1, ft), F32),
                pltpu.VMEM((c2, c1), F32),
                pltpu.VMEM((c2, c2), F32),
                pltpu.VMEM((SLOTS, ROW), F32),
                pltpu.VMEM((c2, ROW), F32),
                pltpu.VMEM((c1, ROW), F32),
            ],
        ),
        compiler_params=pltpu.CompilerParams(
            dimension_semantics=("arbitrary",), vmem_limit_bytes=BLIM * 1024
        ),
        cost_estimate=pl.CostEstimate(
            flops=2 * total * 48000, bytes_accessed=25_000_000, transcendentals=0
        ),
        name="backward",
    )(*scalars, pixels, *saved, *consts)


def from_behind(value, by):
    peers = PIECES
    return lax.ppermute(value, TILE, [(i, (i + by) % peers) for i in range(peers)])


def swap(value, axes):
    return lax.all_to_all(value, axes, 0, 0, tiled=True)


def summed_everywhere(pieces):
    mine = jnp.sum(swap(pieces, TILE), axis=0)
    states = lax.axis_size("z")
    mine = jnp.sum(swap(jnp.broadcast_to(mine[None], (states, 1, PIECE)), ("z",)), axis=0)
    return swap(jnp.broadcast_to(mine[None], (PIECES, 1, PIECE)), TILE)


def on_device(
    bands, block_slot, tile_counties, county_place, label, w_first, taps, w_second, w_third, w_head
):
    pixels = bands[0]
    cty_dev = label.shape[1]
    devices = float(lax.axis_size("z") * PIECES)
    me = (lax.axis_index("x") * 4 + lax.axis_index("y")) * 2 + lax.axis_index("core")
    lists = in_hbm(block_slot, tile_counties, county_place)
    scalars = (*lists, me.astype(jnp.int32)[None, None])
    w2t, wh = w_second.T, w_head[None, :]
    *saved, heads, packet = forward(
        cty_dev, scalars, block_slot, label, pixels, w_first, taps, w2t, w_third, wh
    )
    far = REACH - 1
    packets = [from_behind(packet, -k) if k else packet for k in range(-far, far + 1)]
    grads = chain(saved, w2t, w_third, wh)
    saved = (saved[0], saved[1], *grads)
    rows, county_mean = backward(
        devices, cty_dev, lists[:1], pixels, saved, heads, packets, w_first, taps
    )
    total = summed_everywhere(rows.reshape(PIECES, 1, PIECE))
    count = w_first.size + taps.size + w_second.size + w_third.size + w_head.size
    return county_mean, total.reshape(-1)[:count]


def solution(mesh):
    shape = mesh.devices.shape
    fine = Mesh(mesh.devices.reshape(shape[0], 4, 4, 2), ("z",) + TILE)
    in_specs = (
        P("z", None, TILE),
        P("z", TILE),
        P("z", TILE),
        P("z", None),
        P("z", TILE),
        P(),
        P(),
        P(),
        P(),
        P(),
    )
    return jax.shard_map(
        on_device, mesh=fine, in_specs=in_specs, out_specs=(P("z", TILE), P()), check_vma=False
    )
```

```python
import functools

import jax
import jax.numpy as jnp
from jax import lax
from jax.experimental import pallas as pl
from jax.experimental.pallas import tpu as pltpu
from jax.sharding import Mesh
from jax.sharding import PartitionSpec as P

REACH = 4
ROW = 128
SLOTS = 8
PIECES = 32
PIECE = 1280
F32 = jnp.float32
BF16 = jnp.bfloat16
TILE = ("x", "y", "core")
FPX = 8192
BPX = 8192
WIDTH = 2
BW = 16
CPX = 8192
FLIM = 34000
BLIM = 38000
CLIM = 20000


def mm(left, right):
    return jnp.dot(left, right, preferred_element_type=F32)


def mm_nt(left, right):
    return lax.dot_general(left, right, (((1,), (1,)), ((), ())), preferred_element_type=F32)


def iota(shape, axis):
    return lax.broadcasted_iota(jnp.int32, shape, axis)


def as_column(row, count):
    square = iota((count, count), 0) == iota((count, count), 1)
    return jnp.sum(jnp.where(square, row, 0.0), axis=1, keepdims=True)


def roll_rows(field, by):
    count = field.shape[1] // ROW
    parts = [pltpu.roll(field[:, i * ROW : (i + 1) * ROW], by % ROW, 1) for i in range(count)]
    return parts[0] if count == 1 else jnp.concatenate(parts, axis=1)


def wide(field, count):
    return field if count == 1 else jnp.concatenate([field] * count, axis=1)


def gate(half):
    plus = 1.0 + jnp.tanh(half)
    out = half * plus
    return out, out.astype(BF16), plus.astype(BF16)


def slope(low, plus):
    return plus + low * (2.0 - plus)


def in_hbm(*arrays):
    return tuple(pltpu.with_memory_space_constraint(a, pltpu.HBM) for a in arrays)


def whole(shape):
    zeros = (0,) * len(shape)
    return pl.BlockSpec(shape, lambda i, *s: zeros)


def forward_kernel(
    cty_dev, slots, counties, table, me, x_ref, slotv, label, w1, taps, w2t, w3, wh,
    a1_ref, a2_ref, d3_ref, dh2_ref, p1, heads_ref, packet,
    tapm, w2h, w3h, w3th, whf, whb, p2, acc,
):
    step = pl.program_id(0)
    c2, c1 = w3.shape[0], w2t.shape[0]

    @pl.when(step == 0)
    def _():
        lane = iota((c1, ROW), 1)
        for k in range(3):
            col = jnp.broadcast_to(0.5 * as_column(taps[k : k + 1, :], c1), (c1, ROW))
            if k == 0:
                col = jnp.where(lane > 0, col, 0.0)
            if k == 2:
                col = jnp.where(lane < ROW - 1, col, 0.0)
            tapm[k] = col
        w2h[...] = jnp.transpose(0.5 * w2t[...].astype(F32)).astype(BF16)
        half3 = 0.5 * w3[...].astype(F32)
        w3h[...] = half3.astype(BF16)
        w3th[...] = jnp.transpose(half3).astype(BF16)
        col = jnp.broadcast_to(0.5 * as_column(wh[...].astype(F32), c2), (c2, ROW))
        whf[...] = col
        whb[...] = col.astype(BF16)
        acc[...] = jnp.zeros_like(acc)

    px = x_ref.shape[1]
    spans = [pl.ds(c * WIDTH * ROW, WIDTH * ROW) for c in range(px // (WIDTH * ROW))]
    n = WIDTH
    for at in spans:
        h1 = mm(w1[...], x_ref[:, at])
        s1 = wide(tapm[0], n) * roll_rows(h1, 1) + wide(tapm[1], n) * h1
        s1 = s1 + wide(tapm[2], n) * roll_rows(h1, -1)
        _, a1_ref[:, at], p1[:, at] = gate(s1)
    for at in spans:
        _, a2_ref[:, at], p2[:, at] = gate(mm(w2h[...], a1_ref[:, at]))
    heads = jnp.zeros(acc.shape, F32)
    for c, at in enumerate(spans):
        a2 = a2_ref[:, at]
        out, low, plus = gate(mm(w3h[...], a2))
        d3_ref[:, at] = wide(whb[...], n) * slope(low, plus)
        a3 = (out + a2.astype(F32)).astype(BF16)
        member = []
        for j in range(n):
            slot = slots[0, step * (px // ROW) + c * n + j]
            member.append((iota(acc.shape, 0) == slot).astype(F32).astype(BF16))
        heads = heads + mm_nt(jnp.concatenate(member, axis=1), a3)
    for at in spans:
        back = mm(w3th[...], d3_ref[:, at]) + wide(whf[...], n)
        dh2_ref[:, at] = back.astype(BF16) * slope(a2_ref[:, at], p2[:, at])
    acc[...] += heads

    @pl.when(step == pl.num_programs(0) - 1)
    def _():
        per_slot = acc[0:SLOTS, :]
        heads_ref[...] = per_slot
        sums = jnp.sum(per_slot * wh[...].astype(F32), axis=1, keepdims=True)
        counts = (slotv[...] == iota((SLOTS, slotv.shape[1]), 0)).astype(F32)
        counts = jnp.sum(counts, axis=1, keepdims=True) * float(ROW)
        blank = jnp.zeros((1, ROW), F32)
        codes, spots, lane = blank, blank, iota((1, ROW), 1)
        for s in range(SLOTS):
            place = table[0, counties[0, s]]
            owner = lax.div(place, cty_dev)
            spot = cty_dev * lax.rem(owner - me[0, 0] + PIECES, PIECES) + place - cty_dev * owner
            codes = jnp.where(lane == s, (place + 1).astype(F32), codes)
            spots = jnp.where(lane == s, spot.astype(F32), spots)
        base = jnp.zeros((1, ROW), jnp.int32) + (cty_dev * me[0, 0] + 1)
        own = label[...].astype(F32)
        own = jnp.concatenate([own, jnp.zeros((1, ROW - own.shape[1]), F32)], axis=1)
        slot_lane = iota((SLOTS, ROW), 0) == iota((SLOTS, ROW), 1)
        as_row = lambda col: jnp.sum(jnp.where(slot_lane, col, 0.0), axis=0, keepdims=True)
        packet[...] = jnp.concatenate(
            [as_row(sums), as_row(counts), codes, own, spots, base.astype(F32), blank, blank]
        )


def forward(cty_dev, scalars, slotv, label, pixels, w1, taps, w2t, w3, wh):
    total = pixels.shape[1]
    c1, c2 = w2t.shape[0], w2t.shape[1]
    chans = [c1, c2, c2, c2, c1]
    px = FPX
    scalar_specs = [pl.BlockSpec(memory_space=pltpu.SMEM)] * len(scalars)
    cols = lambda ch: pl.BlockSpec((ch, px), lambda i, *s: (0, i))
    (pixels,) = in_hbm(pixels)
    consts = in_hbm(slotv, label, w1, taps, w2t, w3, wh)
    small = [(SLOTS, c2), (SLOTS, ROW)]
    return pl.pallas_call(
        functools.partial(forward_kernel, cty_dev),
        out_shape=[jax.ShapeDtypeStruct((ch, total), BF16) for ch in chans]
        + [jax.ShapeDtypeStruct(s, F32) for s in small],
        grid_spec=pltpu.PrefetchScalarGridSpec(
            num_scalar_prefetch=0,
            grid=(total // px,),
            in_specs=scalar_specs + [cols(pixels.shape[0])] + [whole(w.shape) for w in consts],
            out_specs=[cols(ch) for ch in chans] + [whole(s) for s in small],
            scratch_shapes=[
                pltpu.VMEM((3, c1, ROW), F32),
                pltpu.VMEM((c2, c1), BF16),
                pltpu.VMEM((c2, c2), BF16),
                pltpu.VMEM((c2, c2), BF16),
                pltpu.VMEM((c2, ROW), F32),
                pltpu.VMEM((c2, ROW), BF16),
                pltpu.VMEM((c2, px), BF16),
                pltpu.VMEM((16, c2), F32),
            ],
        ),
        compiler_params=pltpu.CompilerParams(
            dimension_semantics=("arbitrary",), vmem_limit_bytes=FLIM * 1024
        ),
        cost_estimate=pl.CostEstimate(
            flops=2 * total * 42000, bytes_accessed=25_000_000, transcendentals=total * 320
        ),
        name="forward",
    )(*scalars, pixels, *consts)


def chain_kernel(a1_ref, p1, dh2_ref, w2t, ds_ref, w2th):
    n = WIDTH

    @pl.when(pl.program_id(0) == 0)
    def _():
        w2th[...] = (0.5 * w2t[...].astype(F32)).astype(BF16)

    px = a1_ref.shape[1]
    for c in range(px // (n * ROW)):
        at = pl.ds(c * n * ROW, n * ROW)
        back = mm(w2th[...], dh2_ref[:, at])
        ds_ref[:, at] = back.astype(BF16) * slope(a1_ref[:, at], p1[:, at])


def chain(a1, p1, dh2, w2t):
    c1, total = a1.shape
    px = CPX
    cols = lambda ch: pl.BlockSpec((ch, px), lambda i, *s: (0, i))
    (w2t,) = in_hbm(w2t)
    return pl.pallas_call(
        chain_kernel,
        out_shape=jax.ShapeDtypeStruct((c1, total), BF16),
        grid=(total // px,),
        in_specs=[cols(c1), cols(c1), cols(dh2.shape[0]), whole(w2t.shape)],
        out_specs=cols(c1),
        scratch_shapes=[pltpu.VMEM(w2t.shape, BF16)],
        compiler_params=pltpu.CompilerParams(
            dimension_semantics=("arbitrary",), vmem_limit_bytes=CLIM * 1024
        ),
        cost_estimate=pl.CostEstimate(
            flops=2 * total * 9000, bytes_accessed=12_000_000, transcendentals=0
        ),
        name="chain",
    )(a1, p1, dh2, w2t)


def settle(devices, cty_dev, packets, mean_ref):
    lane = iota((SLOTS, ROW), 1)
    got = jnp.zeros((SLOTS, ROW), F32)
    labels = jnp.zeros((1, ROW), F32)
    far = REACH - 1
    for k, ref in enumerate(packets):
        packet = ref[...]
        moved = pltpu.roll(packet, SLOTS * k, 1) if k else packet
        got = jnp.where((lane >= SLOTS * k) & (lane < SLOTS * (k + 1)), moved, got)
        if k >= far:
            at = cty_dev * (k - far)
            row = packet[3:4, :]
            row = pltpu.roll(row, at, 1) if at else row
            here = lane[0:1, :]
            labels = jnp.where((here >= at) & (here < at + cty_dev), row, labels)
    sums, counts, codes = got[0:1, :], got[1:2, :], got[2:3, :]
    own = packets[far][...]
    code = as_column(own[2:3, :SLOTS], SLOTS)
    spot = as_column(own[4:5, :SLOTS], SLOTS)

    def mean_of(hit):
        total = jnp.sum(jnp.where(hit, sums, 0.0), axis=1, keepdims=True)
        number = jnp.sum(jnp.where(hit, counts, 0.0), axis=1, keepdims=True)
        denom = jnp.maximum(number, 1.0)
        return total / denom, number, denom

    mean, number, denom = mean_of(codes == code)
    target = jnp.sum(jnp.where(lane.astype(F32) == spot, labels, 0.0), axis=1, keepdims=True) * 0.01
    live = jnp.where(number > 0.5, 2.0, 0.0)
    adjoint = live * (mean - target) / (devices * denom)
    owned = iota((16, ROW), 0)
    mine = (codes == owned.astype(F32) + own[5:6, :]) & (owned < cty_dev)
    mean, _, _ = mean_of(mine)
    spread = jnp.sum(jnp.where(owned == iota((16, ROW), 1), mean, 0.0), axis=0, keepdims=True)
    mean_ref[...] = spread[:, :cty_dev]
    return adjoint


def write_flat(after, same, before, second, third, head, w1, taps, lo, hi, rows):
    c1, ft = w1.shape
    cols = [as_column(taps[k : k + 1, :], c1) for k in range(3)]
    first = cols[0] * after + cols[1] * same + cols[2] * before
    lo[0:c1, :] = first[:, :ROW]
    hi[...] = jnp.zeros_like(hi)
    hi[:, 0 : ft - ROW] = first[:, ROW:]
    filled = 15
    lane = iota((8, ROW), 1)
    for p in range(filled):
        src, at = divmod(p * ROW, ft)
        near = pl.ds(src, 8, stride=8)
        piece = jnp.concatenate([lo[near, :], hi[near, :]], axis=1)
        piece = pltpu.roll(piece, (-at) % 256, 1)[:, :ROW] if at else piece[:, :ROW]
        left = ft - at
        if left < ROW:
            far = lo[pl.ds(src + 1, 8, stride=8), :]
            piece = jnp.where(lane < left, piece, pltpu.roll(far, left, 1))
        rows[pl.ds(p, 8, stride=filled), :] = piece
    base = c1 * ft // ROW
    half = ROW // 2
    wf = w1[...].astype(F32)
    t0, t1, t2 = [
        jnp.sum(jnp.transpose(wf * part), axis=0, keepdims=True) for part in (after, same, before)
    ]
    c2 = second.shape[0]
    rows[base : base + 1, :] = jnp.concatenate([t0, t1], axis=1)
    lo[:, 0:half] = second
    even = lo[pl.ds(0, c2 // 2, stride=2), :]
    odd = lo[pl.ds(1, c2 // 2, stride=2), :]
    low = iota((c2, ROW), 1) < half
    rows[base + 2 : base + 1 + c2 // 2, :] = jnp.where(
        low[: c2 // 2 - 1], odd[: c2 // 2 - 1], pltpu.roll(even, half, 1)[1:]
    )
    rows[base + 1 : base + 2, :] = jnp.concatenate([t2, second[0:1]], axis=1)
    mark = base + 1 + c2 // 2
    turned = pltpu.roll(third, half, 1)
    rows[mark : mark + 1, :] = jnp.where(low[0:1], odd[c2 // 2 - 1 :], turned[0:1])
    rows[mark + 1 : mark + c2, :] = jnp.where(low[1:], turned[: c2 - 1], turned[1:])
    turned_head = pltpu.roll(head, half, 1)
    rows[mark + c2 : mark + c2 + 1, :] = jnp.where(low[0:1], turned[c2 - 1 :], turned_head)
    rows[mark + c2 + 1 : mark + c2 + 2, :] = jnp.where(low[0:1], turned_head, 0.0)
    rest = rows.shape[0] - (mark + c2 + 2)
    rows[mark + c2 + 2 :, :] = jnp.zeros((rest, ROW), F32)


def backward_kernel(
    devices, cty_dev, slots, x_ref, a1_ref, a2_ref, d3_ref, dh2_ref, ds_ref, heads, k0, k1, k2, k3, k4, k5, k6, w1, taps,
    rows, mean_ref, g1, g23, gtab, lo, hi, stack, deep,
):
    step = pl.program_id(0)
    c1 = a1_ref.shape[0]
    px = x_ref.shape[1]
    n = BW

    @pl.when(step == 0)
    def _():
        packets = (k0, k1, k2, k3, k4, k5, k6)
        mine = settle(devices, cty_dev, packets, mean_ref)
        gtab[...] = jnp.broadcast_to(mine.astype(BF16).astype(F32), (SLOTS, ROW))
        g1[...] = jnp.zeros_like(g1)
        g23[...] = jnp.zeros_like(g23)

    c2 = d3_ref.shape[0]
    keep = iota((c1, ROW), 1)
    keep_after = (keep < ROW - 1).astype(F32).astype(BF16)
    keep_before = (keep > 0).astype(F32).astype(BF16)
    for r in range(px // ROW):
        at = pl.ds(r * ROW, ROW)
        slot = slots[0, step * (px // ROW) + r]
        scale = jnp.broadcast_to(gtab[pl.ds(slot, 1), :], (16, ROW)).astype(BF16)
        tall = lambda count: jnp.concatenate([scale] * (count // 16), axis=0)
        ds = ds_ref[:, at] * tall(c1)
        stack[0:c1, at] = pltpu.roll(ds, ROW - 1, 1) * keep_after
        stack[c1 : 2 * c1, at] = ds
        stack[2 * c1 :, at] = pltpu.roll(ds, 1, 1) * keep_before
        deep[0:c2, at] = d3_ref[:, at] * tall(c2)
        deep[c2:, at] = dh2_ref[:, at] * tall(c2)
    for c in range(px // (n * ROW)):
        at = pl.ds(c * n * ROW, n * ROW)
        g1[...] += mm_nt(stack[:, at], x_ref[:, at])
        right = jnp.concatenate([a2_ref[:, at], a1_ref[:, at]], axis=0)
        g23[...] += mm_nt(deep[:, at], right)

    @pl.when(step == pl.num_programs(0) - 1)
    def _():
        head = jnp.sum(gtab[...] * heads[...], axis=0, keepdims=True)
        write_flat(
            g1[0:c1], g1[c1 : 2 * c1], g1[2 * c1 :],
            g23[c2:, c2:], g23[0:c2, 0:c2], head, w1, taps, lo, hi, rows,
        )


def backward(devices, cty_dev, scalars, pixels, saved, heads, packets, w1, taps):
    ft, c1, c2 = pixels.shape[0], saved[0].shape[0], saved[1].shape[0]
    px = BPX
    scalar_specs = [pl.BlockSpec(memory_space=pltpu.SMEM)] * len(scalars)
    total = pixels.shape[1]
    cols = lambda ch: pl.BlockSpec((ch, px), lambda i, *s: (0, i))
    (pixels,) = in_hbm(pixels)
    consts = (heads, *packets, *in_hbm(w1, taps))
    return pl.pallas_call(
        functools.partial(backward_kernel, devices, cty_dev),
        out_shape=[
            jax.ShapeDtypeStruct((PIECES * PIECE // ROW, ROW), F32),
            jax.ShapeDtypeStruct((1, cty_dev), F32),
        ],
        grid_spec=pltpu.PrefetchScalarGridSpec(
            num_scalar_prefetch=0,
            grid=(total // px,),
            in_specs=scalar_specs + [cols(v.shape[0]) for v in (pixels, *saved)]
            + [whole(w.shape) for w in consts],
            out_specs=[whole((PIECES * PIECE // ROW, ROW)), whole((1, cty_dev))],
            scratch_shapes=[
                pltpu.VMEM((3 * c1, ft), F32),
                pltpu.VMEM((2 * c2, c1 + c2), F32),
                pltpu.VMEM((SLOTS, ROW), F32),
                pltpu.VMEM((c2, ROW), F32),
                pltpu.VMEM((c1, ROW), F32),
                pltpu.VMEM((3 * c1, px), BF16),
                pltpu.VMEM((2 * c2, px), BF16),
            ],
        ),
        compiler_params=pltpu.CompilerParams(
            dimension_semantics=("arbitrary",), vmem_limit_bytes=BLIM * 1024
        ),
        cost_estimate=pl.CostEstimate(
            flops=2 * total * 48000, bytes_accessed=25_000_000, transcendentals=0
        ),
        name="backward",
    )(*scalars, pixels, *saved, *consts)


def from_behind(value, by):
    peers = PIECES
    return lax.ppermute(value, TILE, [(i, (i + by) % peers) for i in range(peers)])


def swap(value, axes):
    return lax.all_to_all(value, axes, 0, 0, tiled=True)


def summed_everywhere(pieces):
    mine = jnp.sum(swap(pieces, TILE), axis=0)
    states = lax.axis_size("z")
    mine = jnp.sum(swap(jnp.broadcast_to(mine[None], (states, 1, PIECE)), ("z",)), axis=0)
    return swap(jnp.broadcast_to(mine[None], (PIECES, 1, PIECE)), TILE)


def on_device(
    bands, block_slot, tile_counties, county_place, label, w_first, taps, w_second, w_third, w_head
):
    pixels = bands[0]
    cty_dev = label.shape[1]
    devices = float(lax.axis_size("z") * PIECES)
    me = (lax.axis_index("x") * 4 + lax.axis_index("y")) * 2 + lax.axis_index("core")
    lists = in_hbm(block_slot, tile_counties, county_place)
    scalars = (*lists, me.astype(jnp.int32)[None, None])
    w2t, wh = w_second.T, w_head[None, :]
    a1, a2, d3, dh2, p1, heads, packet = forward(
        cty_dev, scalars, block_slot, label, pixels, w_first, taps, w2t, w_third, wh
    )
    far = REACH - 1
    packets = [from_behind(packet, -k) if k else packet for k in range(-far, far + 1)]
    saved = (a1, a2, d3, dh2, chain(a1, p1, dh2, w2t))
    rows, county_mean = backward(
        devices, cty_dev, lists[:1], pixels, saved, heads, packets, w_first, taps
    )
    total = summed_everywhere(rows.reshape(PIECES, 1, PIECE))
    count = w_first.size + taps.size + w_second.size + w_third.size + w_head.size
    return county_mean, total.reshape(-1)[:count]


def solution(mesh):
    shape = mesh.devices.shape
    fine = Mesh(mesh.devices.reshape(shape[0], 4, 4, 2), ("z",) + TILE)
    in_specs = (
        P("z", None, TILE),
        P("z", TILE),
        P("z", TILE),
        P("z", None),
        P("z", TILE),
        P(),
        P(),
        P(),
        P(),
        P(),
    )
    return jax.shard_map(
        on_device, mesh=fine, in_specs=in_specs, out_specs=(P("z", TILE), P()), check_vma=False
    )
```

```python
import functools

import jax
import jax.numpy as jnp
from jax import lax
from jax.experimental import pallas as pl
from jax.experimental.pallas import tpu as pltpu
from jax.sharding import Mesh
from jax.sharding import PartitionSpec as P

REACH = 4
ROW = 128
SLOTS = 8
PIECES = 32
PIECE = 1280
F32 = jnp.float32
BF16 = jnp.bfloat16
TILE = ("x", "y", "core")
FPX = 8192
BPX = 8192
WIDTH = 2
BW = 16
CPX = 8192
FLIM = 34000
BLIM = 38000
CLIM = 20000


def mm(left, right):
    return jnp.dot(left, right, preferred_element_type=F32)


def mm_nt(left, right):
    return lax.dot_general(left, right, (((1,), (1,)), ((), ())), preferred_element_type=F32)


def iota(shape, axis):
    return lax.broadcasted_iota(jnp.int32, shape, axis)


def as_column(row, count):
    square = iota((count, count), 0) == iota((count, count), 1)
    return jnp.sum(jnp.where(square, row, 0.0), axis=1, keepdims=True)


def roll_rows(field, by):
    count = field.shape[1] // ROW
    parts = [pltpu.roll(field[:, i * ROW : (i + 1) * ROW], by % ROW, 1) for i in range(count)]
    return parts[0] if count == 1 else jnp.concatenate(parts, axis=1)


def wide(field, count):
    return field if count == 1 else jnp.concatenate([field] * count, axis=1)


def gate(half):
    plus = 1.0 + jnp.tanh(half)
    out = half * plus
    return out, out.astype(BF16), plus.astype(BF16)


def slope(low, plus):
    return plus + low * (2.0 - plus)


def in_hbm(*arrays):
    return tuple(pltpu.with_memory_space_constraint(a, pltpu.HBM) for a in arrays)


def whole(shape):
    zeros = (0,) * len(shape)
    return pl.BlockSpec(shape, lambda i, *s: zeros)


def forward_kernel(
    cty_dev, slots, counties, table, me, x_ref, slotv, label, w1, taps, w2t, w3, wh,
    a1_ref, a2_ref, d3_ref, dh2_ref, p1, heads_ref, packet,
    tapm, w2h, w3h, w3th, whf, whb, p2, acc,
):
    step = pl.program_id(0)
    c2, c1 = w3.shape[0], w2t.shape[0]

    @pl.when(step == 0)
    def _():
        lane = iota((c1, ROW), 1)
        for k in range(3):
            col = jnp.broadcast_to(0.5 * as_column(taps[k : k + 1, :], c1), (c1, ROW))
            if k == 0:
                col = jnp.where(lane > 0, col, 0.0)
            if k == 2:
                col = jnp.where(lane < ROW - 1, col, 0.0)
            tapm[k] = col
        w2h[...] = jnp.transpose(0.5 * w2t[...].astype(F32)).astype(BF16)
        half3 = 0.5 * w3[...].astype(F32)
        w3h[...] = half3.astype(BF16)
        w3th[...] = jnp.transpose(half3).astype(BF16)
        col = jnp.broadcast_to(0.5 * as_column(wh[...].astype(F32), c2), (c2, ROW))
        whf[...] = col
        whb[...] = col.astype(BF16)
        acc[...] = jnp.zeros_like(acc)

    px = x_ref.shape[1]
    spans = [pl.ds(c * WIDTH * ROW, WIDTH * ROW) for c in range(px // (WIDTH * ROW))]
    n = WIDTH
    for at in spans:
        h1 = mm(w1[...], x_ref[:, at])
        s1 = wide(tapm[0], n) * roll_rows(h1, 1) + wide(tapm[1], n) * h1
        s1 = s1 + wide(tapm[2], n) * roll_rows(h1, -1)
        _, a1_ref[:, at], p1[:, at] = gate(s1)
    for at in spans:
        _, a2_ref[:, at], p2[:, at] = gate(mm(w2h[...], a1_ref[:, at]))
    heads = jnp.zeros(acc.shape, F32)
    for c, at in enumerate(spans):
        a2 = a2_ref[:, at]
        out, low, plus = gate(mm(w3h[...], a2))
        d3_ref[:, at] = wide(whb[...], n) * slope(low, plus)
        a3 = (out + a2.astype(F32)).astype(BF16)
        member = []
        for j in range(n):
            slot = slots[0, step * (px // ROW) + c * n + j]
            member.append((iota(acc.shape, 0) == slot).astype(F32).astype(BF16))
        heads = heads + mm_nt(jnp.concatenate(member, axis=1), a3)
    for at in spans:
        back = mm(w3th[...], d3_ref[:, at]) + wide(whf[...], n)
        dh2_ref[:, at] = back.astype(BF16) * slope(a2_ref[:, at], p2[:, at])
    acc[...] += heads

    @pl.when(step == pl.num_programs(0) - 1)
    def _():
        per_slot = acc[0:SLOTS, :]
        heads_ref[...] = per_slot
        sums = jnp.sum(per_slot * wh[...].astype(F32), axis=1, keepdims=True)
        counts = (slotv[...] == iota((SLOTS, slotv.shape[1]), 0)).astype(F32)
        counts = jnp.sum(counts, axis=1, keepdims=True) * float(ROW)
        blank = jnp.zeros((1, ROW), F32)
        codes, spots, lane = blank, blank, iota((1, ROW), 1)
        for s in range(SLOTS):
            place = table[0, counties[0, s]]
            owner = lax.div(place, cty_dev)
            spot = cty_dev * lax.rem(owner - me[0, 0] + PIECES, PIECES) + place - cty_dev * owner
            codes = jnp.where(lane == s, (place + 1).astype(F32), codes)
            spots = jnp.where(lane == s, spot.astype(F32), spots)
        base = jnp.zeros((1, ROW), jnp.int32) + (cty_dev * me[0, 0] + 1)
        own = label[...].astype(F32)
        own = jnp.concatenate([own, jnp.zeros((1, ROW - own.shape[1]), F32)], axis=1)
        slot_lane = iota((SLOTS, ROW), 0) == iota((SLOTS, ROW), 1)
        as_row = lambda col: jnp.sum(jnp.where(slot_lane, col, 0.0), axis=0, keepdims=True)
        packet[...] = jnp.concatenate(
            [as_row(sums), as_row(counts), codes, own, spots, base.astype(F32), blank, blank]
        )


def forward(cty_dev, scalars, slotv, label, pixels, w1, taps, w2t, w3, wh):
    total = pixels.shape[1]
    c1, c2 = w2t.shape[0], w2t.shape[1]
    chans = [c1, c2, c2, c2, c1]
    px = FPX
    scalar_specs = [pl.BlockSpec(memory_space=pltpu.SMEM)] * len(scalars)
    cols = lambda ch: pl.BlockSpec((ch, px), lambda i, *s: (0, i))
    (pixels,) = in_hbm(pixels)
    consts = in_hbm(slotv, label, w1, taps, w2t, w3, wh)
    small = [(SLOTS, c2), (SLOTS, ROW)]
    return pl.pallas_call(
        functools.partial(forward_kernel, cty_dev),
        out_shape=[jax.ShapeDtypeStruct((ch, total), BF16) for ch in chans]
        + [jax.ShapeDtypeStruct(s, F32) for s in small],
        grid_spec=pltpu.PrefetchScalarGridSpec(
            num_scalar_prefetch=0,
            grid=(total // px,),
            in_specs=scalar_specs + [cols(pixels.shape[0])] + [whole(w.shape) for w in consts],
            out_specs=[cols(ch) for ch in chans] + [whole(s) for s in small],
            scratch_shapes=[
                pltpu.VMEM((3, c1, ROW), F32),
                pltpu.VMEM((c2, c1), BF16),
                pltpu.VMEM((c2, c2), BF16),
                pltpu.VMEM((c2, c2), BF16),
                pltpu.VMEM((c2, ROW), F32),
                pltpu.VMEM((c2, ROW), BF16),
                pltpu.VMEM((c2, px), BF16),
                pltpu.VMEM((16, c2), F32),
            ],
        ),
        compiler_params=pltpu.CompilerParams(
            dimension_semantics=("arbitrary",), vmem_limit_bytes=FLIM * 1024
        ),
        cost_estimate=pl.CostEstimate(
            flops=2 * total * 42000, bytes_accessed=25_000_000, transcendentals=total * 320
        ),
        name="forward",
    )(*scalars, pixels, *consts)


def chain_kernel(a1_ref, p1, dh2_ref, w2t, ds_ref, w2th):
    n = WIDTH

    @pl.when(pl.program_id(0) == 0)
    def _():
        w2th[...] = (0.5 * w2t[...].astype(F32)).astype(BF16)

    px = a1_ref.shape[1]
    for c in range(px // (n * ROW)):
        at = pl.ds(c * n * ROW, n * ROW)
        back = mm(w2th[...], dh2_ref[:, at])
        ds_ref[:, at] = back.astype(BF16) * slope(a1_ref[:, at], p1[:, at])


def chain(a1, p1, dh2, w2t):
    c1, total = a1.shape
    px = CPX
    cols = lambda ch: pl.BlockSpec((ch, px), lambda i, *s: (0, i))
    (w2t,) = in_hbm(w2t)
    return pl.pallas_call(
        chain_kernel,
        out_shape=jax.ShapeDtypeStruct((c1, total), BF16),
        grid=(total // px,),
        in_specs=[cols(c1), cols(c1), cols(dh2.shape[0]), whole(w2t.shape)],
        out_specs=cols(c1),
        scratch_shapes=[pltpu.VMEM(w2t.shape, BF16)],
        compiler_params=pltpu.CompilerParams(
            dimension_semantics=("arbitrary",), vmem_limit_bytes=CLIM * 1024
        ),
        cost_estimate=pl.CostEstimate(
            flops=2 * total * 9000, bytes_accessed=12_000_000, transcendentals=0
        ),
        name="chain",
    )(a1, p1, dh2, w2t)


def settle(devices, cty_dev, packets, mean_ref):
    lane = iota((SLOTS, ROW), 1)
    got = jnp.zeros((SLOTS, ROW), F32)
    labels = jnp.zeros((1, ROW), F32)
    far = REACH - 1
    for k, ref in enumerate(packets):
        packet = ref[...]
        moved = pltpu.roll(packet, SLOTS * k, 1) if k else packet
        got = jnp.where((lane >= SLOTS * k) & (lane < SLOTS * (k + 1)), moved, got)
        if k >= far:
            at = cty_dev * (k - far)
            row = packet[3:4, :]
            row = pltpu.roll(row, at, 1) if at else row
            here = lane[0:1, :]
            labels = jnp.where((here >= at) & (here < at + cty_dev), row, labels)
    sums, counts, codes = got[0:1, :], got[1:2, :], got[2:3, :]
    own = packets[far][...]
    code = as_column(own[2:3, :SLOTS], SLOTS)
    spot = as_column(own[4:5, :SLOTS], SLOTS)

    def mean_of(hit):
        total = jnp.sum(jnp.where(hit, sums, 0.0), axis=1, keepdims=True)
        number = jnp.sum(jnp.where(hit, counts, 0.0), axis=1, keepdims=True)
        denom = jnp.maximum(number, 1.0)
        return total / denom, number, denom

    mean, number, denom = mean_of(codes == code)
    target = jnp.sum(jnp.where(lane.astype(F32) == spot, labels, 0.0), axis=1, keepdims=True) * 0.01
    live = jnp.where(number > 0.5, 2.0, 0.0)
    adjoint = live * (mean - target) / (devices * denom)
    owned = iota((16, ROW), 0)
    mine = (codes == owned.astype(F32) + own[5:6, :]) & (owned < cty_dev)
    mean, _, _ = mean_of(mine)
    spread = jnp.sum(jnp.where(owned == iota((16, ROW), 1), mean, 0.0), axis=0, keepdims=True)
    mean_ref[...] = spread[:, :cty_dev]
    return adjoint


def write_flat(after, same, before, second, third, head, w1, taps, lo, hi, rows):
    c1, ft = w1.shape
    cols = [as_column(taps[k : k + 1, :], c1) for k in range(3)]
    first = cols[0] * after + cols[1] * same + cols[2] * before
    lo[0:c1, :] = first[:, :ROW]
    hi[...] = jnp.zeros_like(hi)
    hi[0:c1, 0 : ft - ROW] = first[:, ROW:]
    filled = 15
    lane = iota((8, ROW), 1)
    for p in range(filled):
        src, at = divmod(p * ROW, ft)
        near = pl.ds(src, 8, stride=8)
        piece = jnp.concatenate([lo[near, :], hi[near, :]], axis=1)
        piece = pltpu.roll(piece, (-at) % 256, 1)[:, :ROW] if at else piece[:, :ROW]
        left = ft - at
        if left < ROW:
            far = lo[pl.ds(src + 1, 8, stride=8), :]
            piece = jnp.where(lane < left, piece, pltpu.roll(far, left, 1))
        rows[pl.ds(p, 8, stride=filled), :] = piece
    base = c1 * ft // ROW
    half = ROW // 2
    wf = w1[...].astype(F32)
    t0, t1, t2 = [
        jnp.sum(jnp.transpose(wf * part), axis=0, keepdims=True) for part in (after, same, before)
    ]
    c2 = second.shape[0]
    rows[base : base + 1, :] = jnp.concatenate([t0, t1], axis=1)
    lo[0:c2, 0:half] = second
    even = lo[pl.ds(0, c2 // 2, stride=2), :]
    odd = lo[pl.ds(1, c2 // 2, stride=2), :]
    low = iota((c2, ROW), 1) < half
    rows[base + 2 : base + 1 + c2 // 2, :] = jnp.where(
        low[: c2 // 2 - 1], odd[: c2 // 2 - 1], pltpu.roll(even, half, 1)[1:]
    )
    rows[base + 1 : base + 2, :] = jnp.concatenate([t2, second[0:1]], axis=1)
    mark = base + 1 + c2 // 2
    turned = pltpu.roll(third, half, 1)
    rows[mark : mark + 1, :] = jnp.where(low[0:1], odd[c2 // 2 - 1 :], turned[0:1])
    rows[mark + 1 : mark + c2, :] = jnp.where(low[1:], turned[: c2 - 1], turned[1:])
    turned_head = pltpu.roll(head, half, 1)
    rows[mark + c2 : mark + c2 + 1, :] = jnp.where(low[0:1], turned[c2 - 1 :], turned_head)
    rows[mark + c2 + 1 : mark + c2 + 2, :] = jnp.where(low[0:1], turned_head, 0.0)
    rest = rows.shape[0] - (mark + c2 + 2)
    rows[mark + c2 + 2 :, :] = jnp.zeros((rest, ROW), F32)


def backward_kernel(
    devices, cty_dev, slots, x_ref, a1_ref, a2_ref, d3_ref, dh2_ref, ds_ref, heads, k0, k1, k2, k3, k4, k5, k6, w1, taps,
    rows, mean_ref, g1, g23, gtab, lo, hi, stack, right,
):
    step = pl.program_id(0)
    c1 = a1_ref.shape[0]
    px = x_ref.shape[1]
    n = BW

    @pl.when(step == 0)
    def _():
        packets = (k0, k1, k2, k3, k4, k5, k6)
        mine = settle(devices, cty_dev, packets, mean_ref)
        gtab[...] = jnp.broadcast_to(mine.astype(BF16).astype(F32), (SLOTS, ROW))
        g1[...] = jnp.zeros_like(g1)
        g23[...] = jnp.zeros_like(g23)

    c2 = d3_ref.shape[0]
    keep = iota((c1, ROW), 1)
    keep_after = (keep < ROW - 1).astype(F32).astype(BF16)
    keep_before = (keep > 0).astype(F32).astype(BF16)
    for r in range(px // ROW):
        at = pl.ds(r * ROW, ROW)
        slot = slots[0, step * (px // ROW) + r]
        scale = jnp.broadcast_to(gtab[pl.ds(slot, 1), :], (16, ROW)).astype(BF16)
        tall = lambda count: jnp.concatenate([scale] * (count // 16), axis=0)
        ds = ds_ref[:, at] * tall(c1)
        stack[0:c1, at] = pltpu.roll(ds, ROW - 1, 1) * keep_after
        stack[c1 : 2 * c1, at] = ds
        stack[2 * c1 :, at] = pltpu.roll(ds, 1, 1) * keep_before
        right[0:c2, at] = a2_ref[:, at] * tall(c2)
        right[c2:, at] = a1_ref[:, at] * tall(c1)
    for c in range(px // (n * ROW)):
        at = pl.ds(c * n * ROW, n * ROW)
        g1[...] += mm_nt(stack[:, at], x_ref[:, at])
        deep = jnp.concatenate([d3_ref[:, at], dh2_ref[:, at]], axis=0)
        g23[...] += mm_nt(deep, right[:, at])

    @pl.when(step == pl.num_programs(0) - 1)
    def _():
        head = jnp.sum(gtab[...] * heads[...], axis=0, keepdims=True)
        write_flat(
            g1[0:c1], g1[c1 : 2 * c1], g1[2 * c1 :],
            g23[c2:, c2:], g23[0:c2, 0:c2], head, w1, taps, lo, hi, rows,
        )


def backward(devices, cty_dev, scalars, pixels, saved, heads, packets, w1, taps):
    ft, c1, c2 = pixels.shape[0], saved[0].shape[0], saved[1].shape[0]
    px = BPX
    scalar_specs = [pl.BlockSpec(memory_space=pltpu.SMEM)] * len(scalars)
    total = pixels.shape[1]
    cols = lambda ch: pl.BlockSpec((ch, px), lambda i, *s: (0, i))
    (pixels,) = in_hbm(pixels)
    consts = (heads, *packets, *in_hbm(w1, taps))
    return pl.pallas_call(
        functools.partial(backward_kernel, devices, cty_dev),
        out_shape=[
            jax.ShapeDtypeStruct((PIECES * PIECE // ROW, ROW), F32),
            jax.ShapeDtypeStruct((1, cty_dev), F32),
        ],
        grid_spec=pltpu.PrefetchScalarGridSpec(
            num_scalar_prefetch=0,
            grid=(total // px,),
            in_specs=scalar_specs + [cols(v.shape[0]) for v in (pixels, *saved)]
            + [whole(w.shape) for w in consts],
            out_specs=[whole((PIECES * PIECE // ROW, ROW)), whole((1, cty_dev))],
            scratch_shapes=[
                pltpu.VMEM((3 * c1, ft), F32),
                pltpu.VMEM((2 * c2, c1 + c2), F32),
                pltpu.VMEM((SLOTS, ROW), F32),
                pltpu.VMEM((c2 + 8, ROW), F32),
                pltpu.VMEM((c1 + 8, ROW), F32),
                pltpu.VMEM((3 * c1, px), BF16),
                pltpu.VMEM((c1 + c2, px), BF16),
            ],
        ),
        compiler_params=pltpu.CompilerParams(
            dimension_semantics=("arbitrary",), vmem_limit_bytes=BLIM * 1024
        ),
        cost_estimate=pl.CostEstimate(
            flops=2 * total * 48000, bytes_accessed=25_000_000, transcendentals=0
        ),
        name="backward",
    )(*scalars, pixels, *saved, *consts)


def from_behind(value, by):
    peers = PIECES
    return lax.ppermute(value, TILE, [(i, (i + by) % peers) for i in range(peers)])


def swap(value, axes):
    return lax.all_to_all(value, axes, 0, 0, tiled=True)


def summed_everywhere(pieces):
    mine = jnp.sum(swap(pieces, TILE), axis=0)
    states = lax.axis_size("z")
    mine = jnp.sum(swap(jnp.broadcast_to(mine[None], (states, 1, PIECE)), ("z",)), axis=0)
    return swap(jnp.broadcast_to(mine[None], (PIECES, 1, PIECE)), TILE)


def on_device(
    bands, block_slot, tile_counties, county_place, label, w_first, taps, w_second, w_third, w_head
):
    pixels = bands[0]
    cty_dev = label.shape[1]
    devices = float(lax.axis_size("z") * PIECES)
    me = (lax.axis_index("x") * 4 + lax.axis_index("y")) * 2 + lax.axis_index("core")
    lists = in_hbm(block_slot, tile_counties, county_place)
    scalars = (*lists, me.astype(jnp.int32)[None, None])
    w2t, wh = w_second.T, w_head[None, :]
    a1, a2, d3, dh2, p1, heads, packet = forward(
        cty_dev, scalars, block_slot, label, pixels, w_first, taps, w2t, w_third, wh
    )
    far = REACH - 1
    packets = [from_behind(packet, -k) if k else packet for k in range(-far, far + 1)]
    saved = (a1, a2, d3, dh2, chain(a1, p1, dh2, w2t))
    rows, county_mean = backward(
        devices, cty_dev, lists[:1], pixels, saved, heads, packets, w_first, taps
    )
    total = summed_everywhere(rows.reshape(PIECES, 1, PIECE))
    count = w_first.size + taps.size + w_second.size + w_third.size + w_head.size
    return county_mean, total.reshape(-1)[:count]


def solution(mesh):
    shape = mesh.devices.shape
    fine = Mesh(mesh.devices.reshape(shape[0], 4, 4, 2), ("z",) + TILE)
    in_specs = (
        P("z", None, TILE),
        P("z", TILE),
        P("z", TILE),
        P("z", None),
        P("z", TILE),
        P(),
        P(),
        P(),
        P(),
        P(),
    )
    return jax.shard_map(
        on_device, mesh=fine, in_specs=in_specs, out_specs=(P("z", TILE), P()), check_vma=False
    )
```
